256 devices in a mesh: row: 8 (over y, core), col: 32 (over z, x).
Axes of the slice: x: 4, y: 4, z: 8, core: 2. Of those that a mesh axis runs over, the one named last changes fastest.
Arguments:
- row_points: float32 [64, 16384], P(None, 'row'), may hold values from -6 to 6
- panel_points: float32 [64, 1024], P(None, 'col'), may hold values from -6 to 6
- scales: float32 [64], replicated, may hold values from 0.005 to 0.03
Outputs:
- diag_factor: float32 [1024, 1024], P('row', 'col')
- panel_factor_t: float32 [1024, 16384], P('col', 'row')
- updated_ahead_t: float32 [1024, 16384], P('col', 'row')
The draws below stay inside these ranges and needn't reach their ends.
All inputs are finite; a program needn't handle non-finite values.
Results may differ from the reference program's by a relative error of at most 0.0003.
Values sent between devices are 32-bit elements; how exact they have to be, the bound alone decides.
No kernel may reach another device: no remote copies, remote signals or barrier semaphores. Data moves between devices by JAX's collectives and lax.ppermute only.
A program may use at most 128 MiB of HBM per device.

```python
import math
import jax
import jax.numpy as jnp
from jax import lax

F = 64
B = 1024
M = 16384


def block_levels(key, dims, pieces, least, largest):
    loudness = 1.0
    for position, blocks in pieces:
        draws = jax.random.uniform(jax.random.fold_in(jax.random.fold_in(key, 6), position), (blocks,), jnp.float32, least / len(pieces), largest / len(pieces))
        loudness = loudness * jnp.repeat(jnp.exp(draws), dims[position] // blocks).reshape((-1,) + (1,) * (len(dims) - 1 - position))
    return loudness


def scatter_about(own_key, extent, spread, limit, pieces=(), kind=jnp.bfloat16):
    result = jax.random.normal(own_key, extent, jnp.float32) * spread
    if len(pieces) > 0:
        result = block_levels(own_key, extent, pieces, -0.22, 0.18) * result
    return jnp.clip(result, min=-limit, max=limit).astype(kind)


def setup_inputs(seed: int = 0) -> dict:
    streams_of = jax.random.split(jax.random.key(seed), 4)
    return {
        "row_points": scatter_about(streams_of[0], (F, M), 1.0, 6.0, ((1, 8),), jnp.float32),
        "panel_points": scatter_about(streams_of[1], (F, B), 1.0, 6.0, ((1, 32),), jnp.float32),
        "scales": jnp.clip(jnp.exp(jax.random.uniform(streams_of[2], (F,), jnp.float32, math.log(0.005), math.log(0.03))), 0.005, 0.03),
    }


RIDGE = 0.5

def kernel_block(sources, targets, scales):
    weighted = sources * scales[:, None]
    source_sq = jnp.sum(weighted * sources, axis=0)
    target_sq = jnp.sum(targets * targets * scales[:, None], axis=0)
    cross = lax.dot_general(weighted.astype(jnp.float32), targets.astype(jnp.float32), (((0,), (0,)), ((), ())), precision=lax.Precision.HIGHEST, preferred_element_type=jnp.float32)
    return jnp.exp(2.0 * cross - source_sq[:, None] - target_sq[None, :])

def reference(row_points, panel_points, scales):
    diag_block = kernel_block(panel_points, panel_points, scales) + RIDGE * jnp.eye(B, dtype=jnp.float32)
    diag_factor = jnp.linalg.cholesky(diag_block)
    panel_kernel = kernel_block(panel_points, row_points, scales)
    panel_factor = lax.linalg.triangular_solve(diag_factor, panel_kernel, left_side=True, lower=True)
    look_points = row_points[:, :B]
    cross_term = lax.dot_general(panel_factor[:, :B].astype(jnp.float32), panel_factor.astype(jnp.float32), (((0,), (0,)), ((), ())), precision=lax.Precision.HIGHEST, preferred_element_type=jnp.float32)
    updated = kernel_block(look_points, row_points, scales) - cross_term
    return (diag_factor, panel_factor, updated)
```

```python
import functools

import jax
import jax.numpy as jnp
from jax import lax
from jax.experimental import pallas as pl
from jax.experimental.pallas import tpu as pltpu
from jax.sharding import PartitionSpec as P

B = 1024
F = 64
RIDGE = 0.5
TILE = 128
REG = (8, 128)
NN = ((1,), (0,))
TN = ((0,), (0,))
NT = ((1,), (1,))


def mm(a, b, dims):
    return lax.dot_general(
        a, b, (dims, ((), ())), precision=lax.Precision.HIGHEST, preferred_element_type=jnp.float32
    )


def row_all(x, i):
    return jnp.broadcast_to(x[i : i + 1, :], REG)


def col_all(x, j):
    return jnp.broadcast_to(x[:, j : j + 1], REG)


def factor_tile(R):
    n = len(R)
    R = list(R)
    sub = lax.broadcasted_iota(jnp.int32, REG, 0)
    lane = lax.broadcasted_iota(jnp.int32, REG, 1)
    E = [jnp.where(lane == sub + 8 * q, 1.0, 0.0).astype(jnp.float32) for q in range(n)]
    U, G = [], []
    for p in range(n):
        C = {q: [col_all(R[q], 8 * p + k) for k in range(8)] for q in range(p, n)}
        d = [[row_all(C[p][k], i) if i >= k else None for k in range(8)] for i in range(8)]
        r = [row_all(R[p], i) for i in range(8)]
        e = [row_all(E[p], i) for i in range(8)]
        for s in range(8):
            rs = lax.rsqrt(d[s][s])
            l = {k: d[k][s] * rs for k in range(s + 1, 8)}
            for k in range(s + 1, 8):
                for m in range(s + 1, k + 1):
                    d[k][m] = d[k][m] - l[k] * l[m]
            r[s] = r[s] * rs
            e[s] = e[s] * rs
            for k in range(s + 1, 8):
                r[k] = r[k] - l[k] * r[s]
                e[k] = e[k] - l[k] * e[s]
            for q in range(p + 1, n):
                C[q][s] = C[q][s] * rs
                for k in range(s + 1, 8):
                    C[q][k] = C[q][k] - l[k] * C[q][s]
        for q in range(p + 1, n):
            for s in range(8):
                R[q] = R[q] - C[q][s] * r[s]
                E[q] = E[q] - C[q][s] * e[s]
        u, g = r[7], e[7]
        for s in range(6, -1, -1):
            u = jnp.where(sub == s, r[s], u)
            g = jnp.where(sub == s, e[s], g)
        U.append(u)
        G.append(g)
    return U, G


def unpack_points(packed):
    n = packed.shape[0] // 16
    halves = packed.reshape(n, 16, 2 * F)
    return jnp.concatenate([halves[:, :, :F], halves[:, :, F:]], axis=1).reshape(32 * n, F)


def factor_kernel(where_ref, pan_ref, look_ref, scales_ref, diag_ref, z_ref, a_ref, g_ref, b_ref):
    nb = B // TILE
    col, row = where_ref[0], where_ref[1]
    scales = scales_ref[...]
    points = unpack_points(pan_ref[...])
    weighted = points * scales
    look = unpack_points(look_ref[...])
    others = jnp.concatenate([points, look, jnp.zeros((TILE - look.shape[0], F), jnp.float32)], axis=0)
    ones = jnp.ones((8, F), jnp.float32)
    other_sq = mm(ones, others * others * scales, NT)[0:1, :]
    for i in range(nb):
        w = weighted[i * TILE : (i + 1) * TILE]
        sq = jnp.sum(w * points[i * TILE : (i + 1) * TILE], axis=1, keepdims=True)
        cross = mm(w, others, NT)
        block = jnp.exp(2.0 * cross - sq - other_sq)
        rid = lax.broadcasted_iota(jnp.int32, block.shape, 0) + i * TILE
        cid = lax.broadcasted_iota(jnp.int32, block.shape, 1)
        a_ref[i * TILE : (i + 1) * TILE, :] = jnp.where(rid == cid, block + RIDGE, block)

    width = 2 * TILE

    def step(k, carry):
        at = pl.multiple_of(k * TILE, TILE)
        here = pl.ds(at, TILE)
        big = k // 2
        R = [a_ref[pl.ds(at + 8 * q, 8), here] for q in range(TILE // 8)]
        U, G = factor_tile(R)
        g = jnp.concatenate(G, axis=0)
        g_ref[k] = g
        u = jnp.concatenate(U, axis=0)

        def panel(j, carry):
            cols = pl.ds(pl.multiple_of(j * width, width), width)
            a_ref[here, cols] = mm(g, a_ref[here, cols], NN)
            return carry

        lax.fori_loop(big, B // width, panel, 0)
        a_ref[here, B : B + TILE] = mm(g, a_ref[here, B : B + TILE], NN)
        a_ref[here, here] = u

        @pl.when(k % 2 == 0)
        def _():
            after = pl.ds(pl.multiple_of(at + TILE, TILE), TILE)
            side = a_ref[here, after]

            def update(j, carry):
                cols = pl.ds(pl.multiple_of(j * width, width), width)
                a_ref[after, cols] = a_ref[after, cols] - mm(side, a_ref[here, cols], TN)
                return carry

            lax.fori_loop(big, B // width, update, 0)
            a_ref[after, B : B + TILE] = a_ref[after, B : B + TILE] - mm(side, a_ref[here, B : B + TILE], TN)

        @pl.when(k % 2 == 1)
        def _():
            rows = pl.ds(pl.multiple_of(big * width, width), width)

            def update_rows(i, carry):
                dest = pl.ds(pl.multiple_of(i * width, width), width)
                side = a_ref[rows, dest]

                def update(j, carry):
                    cols = pl.ds(pl.multiple_of(j * width, width), width)
                    a_ref[dest, cols] = a_ref[dest, cols] - mm(side, a_ref[rows, cols], TN)
                    return carry

                lax.fori_loop(i, B // width, update, 0)
                a_ref[dest, B : B + TILE] = a_ref[dest, B : B + TILE] - mm(side, a_ref[rows, B : B + TILE], TN)
                return carry

            lax.fori_loop(big + 1, B // width, update_rows, 0)

        return carry

    lax.fori_loop(0, nb, step, 0)

    share = 32
    for k in range(nb):
        cols = slice(k * TILE, (k + 1) * TILE)
        r = lax.broadcasted_iota(jnp.int32, (share, TILE), 0) + col * share
        c = lax.broadcasted_iota(jnp.int32, (share, TILE), 1) + k * TILE
        b_ref[0:share, cols] = jnp.where(r == c, 1.0, 0.0).astype(jnp.float32)
        b_ref[share : 2 * share, cols] = a_ref[cols, B : B + TILE].T[0:share, :]
    for k in range(nb - 1, -1, -1):
        cols = slice(k * TILE, (k + 1) * TILE)
        z = mm(b_ref[:, cols], g_ref[k], NN)
        z_ref[:, cols] = z
        if k > 0:
            b_ref[:, 0 : k * TILE] = b_ref[:, 0 : k * TILE] - mm(z, a_ref[0 : k * TILE, cols], NT)

    own = pl.ds(pl.multiple_of(col * share, share), share)
    to = pl.multiple_of(row * TILE, TILE)
    tile = a_ref[own, pl.ds(to, TILE)]
    r = lax.broadcasted_iota(jnp.int32, (share, TILE), 0) + col * share
    c = lax.broadcasted_iota(jnp.int32, (share, TILE), 1) + to
    diag_ref[...] = jnp.where(c >= r, tile, 0.0).T


def rows_kernel(z_ref, pan_ref, look_ref, scales_ref, rows_ref, weight_ref, panel_ref, update_ref):
    scales = scales_ref[...]
    points = unpack_points(pan_ref[...])
    weighted = points * scales
    look = unpack_points(look_ref[...])
    look_weighted = look * scales
    rows = rows_ref[...]
    row_sq = jnp.sum(rows * rows * weight_ref[...], axis=0, keepdims=True)
    sq = jnp.sum(weighted * points, axis=1, keepdims=True)
    look_sq = jnp.sum(look_weighted * look, axis=1, keepdims=True)
    kernel = jnp.exp(2.0 * mm(weighted, rows, NN) - sq - row_sq)
    both = mm(z_ref[...], kernel, NN)
    look_rows = jnp.exp(2.0 * mm(look_weighted, rows, NN) - look_sq - row_sq)
    panel_ref[...] = both[0:32]
    update_ref[...] = look_rows - both[32:64]


def pack(points):
    rows = points.T
    return jnp.concatenate([rows[0:16], rows[16:32]], axis=1)


def local(where, panel, look, scales, row_points):
    share = 2 * look.shape[0]
    rows_dev = row_points.shape[1]
    scales_row = scales.reshape(1, F)
    scales_col = jnp.broadcast_to(scales.reshape(F, 1), (F, 128))[:, :1]
    vmem = pl.BlockSpec(memory_space=pltpu.VMEM)
    diag, z = pl.pallas_call(
        factor_kernel,
        out_shape=(
            jax.ShapeDtypeStruct((B // 8, share), jnp.float32),
            jax.ShapeDtypeStruct((2 * share, B), jnp.float32),
        ),
        in_specs=[pl.BlockSpec(memory_space=pltpu.SMEM), vmem, vmem, vmem],
        out_specs=(vmem, vmem),
        scratch_shapes=[
            pltpu.VMEM((B, B + TILE), jnp.float32),
            pltpu.VMEM((B // TILE, TILE, TILE), jnp.float32),
            pltpu.VMEM((2 * share, B), jnp.float32),
        ],
        name="factor",
    )(where, panel, look, scales_row)
    tile = 256
    fixed = lambda shape: pl.BlockSpec(shape, lambda j: (0, 0))
    cols = lambda n: pl.BlockSpec((n, tile), lambda j: (0, j))
    panel_tile, updated = pl.pallas_call(
        rows_kernel,
        grid=(rows_dev // tile,),
        out_shape=(
            jax.ShapeDtypeStruct((share, rows_dev), jnp.float32),
            jax.ShapeDtypeStruct((share, rows_dev), jnp.float32),
        ),
        in_specs=[fixed((2 * share, B)), fixed((B // 2, 2 * F)), fixed((share // 2, 2 * F)), fixed((1, F)), cols(F), fixed((F, 1))],
        out_specs=(cols(share), cols(share)),
        name="rows",
    )(z, panel, look, scales_row, row_points, scales_col)
    return (diag, panel_tile, updated)


def body(row_points, panel_points, scales):
    n_col = lax.axis_size("col")
    n_row = lax.axis_size("row")
    col = lax.axis_index("col")
    row = lax.axis_index("row")
    share = B // n_col
    rows_dev = row_points.shape[1]
    first = col * share
    look = pack(lax.dynamic_slice_in_dim(row_points, first % rows_dev, share, 1))
    look_all = lax.all_to_all(jnp.broadcast_to(look, (n_row,) + look.shape), "row", 0, 0, tiled=True)
    look = lax.dynamic_index_in_dim(look_all, first // rows_dev, 0, keepdims=False)
    own = pack(panel_points)
    panel = lax.all_to_all(jnp.broadcast_to(own, (n_col,) + own.shape), "col", 0, 0, tiled=True)
    panel = panel.reshape(B // 2, 2 * F)
    where = jnp.stack([col, row]).astype(jnp.int32)
    return local(where, panel, look, scales, row_points)


def solution(mesh):
    return jax.shard_map(
        body,
        mesh=mesh,
        in_specs=(P(None, "row"), P(None, "col"), P()),
        out_specs=(P("row", "col"), P("col", "row"), P("col", "row")),
        check_vma=False,
    )
```

```python
import functools

import jax
import jax.numpy as jnp
from jax import lax
from jax.experimental import pallas as pl
from jax.experimental.pallas import tpu as pltpu
from jax.sharding import PartitionSpec as P

B = 1024
F = 64
RIDGE = 0.5
TILE = 128
REG = (8, 128)
NN = ((1,), (0,))
TN = ((0,), (0,))
NT = ((1,), (1,))


def mm(a, b, dims):
    return lax.dot_general(
        a, b, (dims, ((), ())), precision=lax.Precision.HIGHEST, preferred_element_type=jnp.float32
    )


def row_all(x, i):
    return jnp.broadcast_to(x[i : i + 1, :], REG)


def col_all(x, j):
    return jnp.broadcast_to(x[:, j : j + 1], REG)


def tree_sum(xs):
    xs=list(xs)
    while len(xs)>1:
        xs=[xs[i]+xs[i+1] if i+1<len(xs) else xs[i] for i in range(0,len(xs),2)]
    return xs[0]

def small_chol(d):
    d=[list(x) for x in d]
    rs=[None]*8; l=[[None]*8 for _ in range(8)]
    for s in range(8):
        rs[s]=lax.rsqrt(d[s][s])
        for k in range(s+1,8): l[k][s]=d[k][s]*rs[s]
        for k in range(s+1,8):
            for m in range(s+1,k+1):
                d[k][m]=d[k][m]-l[k][s]*l[m][s]
    return rs,l
def forward(x,rs,l):
    x=list(x)
    for s in range(8):
        x[s]=x[s]*rs[s]
        for k in range(s+1,8): x[k]=x[k]-l[k][s]*x[s]
    return x
def backward(x,rs,l):
    x=list(x)
    for s in range(7,-1,-1):
        x[s]=x[s]*rs[s]
        for k in range(s): x[k]=x[k]-l[s][k]*x[s]
    return x

def factor_tile(W, zero):
    n=len(W); W=list(W)
    sub=lax.broadcasted_iota(jnp.int32,REG,0); lane=lax.broadcasted_iota(jnp.int32,REG,1)
    G=[None]*n
    def entries(cols): return [[row_all(cols[k],i) if i>=k else None for k in range(8)] for i in range(8)]
    def finish(p, rs, l):
        mine=lax.shift_right_logical(lane,3)==p
        w=jnp.where(mine, jnp.where(lane-8*p==sub,1.0,0.0).astype(jnp.float32), W[p])
        w=forward([row_all(w,s) for s in range(8)],rs,l)
        g=w[7]
        for s in range(6,-1,-1): g=jnp.where(sub==s,w[s],g)
        G[p]=jnp.where(lane<8*(p+1),g,0.0)
        return mine,w
    for t in range(n//2):
        p0,p1=2*t,2*t+1
        c0={q:[col_all(W[q],8*p0+k) for k in range(8)] for q in range(p0,n)}
        d1=[col_all(W[p1],8*p1+k) for k in range(8)]
        rs,l=small_chol(entries([x+zero for x in c0[p0]]))
        x=forward(c0[p1],rs,l)
        d1=[d1[k]-tree_sum([x[s]*row_all(x[s],k) for s in range(8)]) for k in range(8)]
        mine,w=finish(p0,rs,l)
        W[p1]=jnp.where(mine,0.0,W[p1])-tree_sum([x[s]*w[s] for s in range(8)])
        v=backward(w,rs,l)
        for q in range(p1+1,n):
            W[q]=jnp.where(mine,0.0,W[q])-tree_sum([c0[q][s]*v[s] for s in range(8)])
        rs,l=small_chol(entries(d1))
        c1={q:[col_all(W[q],8*p1+k) for k in range(8)] for q in range(p1+1,n)}
        mine,w=finish(p1,rs,l)
        v=backward(w,rs,l)
        for q in range(p1+1,n):
            W[q]=jnp.where(mine,0.0,W[q])-tree_sum([c1[q][s]*v[s] for s in range(8)])
    return G

def unpack_points(packed):
    n = packed.shape[0] // 16
    halves = packed.reshape(n, 16, 2 * F)
    return jnp.concatenate([halves[:, :, :F], halves[:, :, F:]], axis=1).reshape(32 * n, F)


def split(x):
    high = x.astype(jnp.bfloat16)
    rest = x - high.astype(jnp.float32)
    middle = rest.astype(jnp.bfloat16)
    low = (rest - middle.astype(jnp.float32)).astype(jnp.bfloat16)
    return high, middle, low


def spread_terms(parts, order, values, axis):
    shape = list(parts[0].shape)
    shape[axis] = TILE
    place = lax.broadcasted_iota(jnp.int32, shape, axis)
    tail = jnp.zeros(shape, jnp.float32)
    for i, v in enumerate(values):
        tail = jnp.where(place == i, v, tail)
    return jnp.concatenate([parts[i] for i in order] + [tail.astype(jnp.bfloat16)], axis=axis)


def as_float(parts):
    return [p.astype(jnp.float32) for p in parts]


LEFT = (0, 0, 1, 0, 1, 2)
RIGHT = (0, 1, 0, 2, 1, 0)


def left_terms(points, scales):
    weighted = points * scales
    sq = jnp.sum(weighted * points, axis=1, keepdims=True)
    return spread_terms(split(2.0 * weighted), LEFT, as_float(split(-sq)) + [1.0, 1.0, 1.0], 1)


def right_terms(points, sq, axis):
    return spread_terms(split(points), RIGHT, [1.0, 1.0, 1.0] + as_float(split(-sq)), axis)


def dot16(a, b, dims):
    return lax.dot_general(a, b, (dims, ((), ())), preferred_element_type=jnp.float32)


def factor_kernel(where_ref, pan_ref, look_ref, scales_ref, zero_ref, diag_ref, z_ref, left_ref, a_ref, g_ref, b_ref, right_ref):
    nb = B // TILE
    col, row = where_ref[0], where_ref[1]
    scales = scales_ref[...]
    points = unpack_points(pan_ref[...])
    look = unpack_points(look_ref[...])
    share = look.shape[0]
    left_ref[0:B] = left_terms(points, scales)
    left_ref[B : B + share] = left_terms(look, scales)
    others = jnp.concatenate([points, look, jnp.zeros((TILE - share, F), jnp.float32)], axis=0)
    right_ref[...] = right_terms(others, jnp.sum(others * others * scales, axis=1, keepdims=True), 1)
    for i in range(nb):
        at = slice(i * TILE, (i + 1) * TILE)
        block = jnp.exp(dot16(left_ref[at], right_ref[i * TILE :], NT))
        a_ref[at, i * TILE :] = block
        rid = lax.broadcasted_iota(jnp.int32, (TILE, TILE), 0)
        cid = lax.broadcasted_iota(jnp.int32, (TILE, TILE), 1)
        a_ref[at, at] = jnp.where(rid == cid, block[:, 0:TILE] + RIDGE, block[:, 0:TILE])
        if i % 2 == 1:
            a_ref[at, (i - 1) * TILE : i * TILE] = jnp.zeros((TILE, TILE), jnp.float32)

    width = 2 * TILE

    def step(k, carry):
        at = pl.multiple_of(k * TILE, TILE)
        here = pl.ds(at, TILE)
        big = k // 2
        G = factor_tile([a_ref[pl.ds(at + 8 * q, 8), here] for q in range(TILE // 8)], zero_ref[...])
        for q in range(TILE // 8):
            g_ref[k, 8 * q : 8 * q + 8, :] = G[q]
        g = g_ref[k]

        def panel(j, carry):
            cols = pl.ds(pl.multiple_of(j * width, width), width)
            a_ref[here, cols] = mm(g, a_ref[here, cols], NN)
            return carry

        lax.fori_loop(big, B // width, panel, 0)
        a_ref[here, B : B + TILE] = mm(g, a_ref[here, B : B + TILE], NN)

        @pl.when(k % 2 == 0)
        def _():
            after = pl.ds(pl.multiple_of(at + TILE, TILE), TILE)
            side = a_ref[here, after]

            def update(j, carry):
                cols = pl.ds(pl.multiple_of(j * width, width), width)
                a_ref[after, cols] = a_ref[after, cols] - mm(side, a_ref[here, cols], TN)
                return carry

            lax.fori_loop(big, B // width, update, 0)
            a_ref[after, B : B + TILE] = a_ref[after, B : B + TILE] - mm(side, a_ref[here, B : B + TILE], TN)

        @pl.when(k % 2 == 1)
        def _():
            rows = pl.ds(pl.multiple_of(big * width, width), width)

            def update_rows(i, carry):
                dest = pl.ds(pl.multiple_of(i * width, width), width)
                side = a_ref[rows, dest]

                def update(j, carry):
                    cols = pl.ds(pl.multiple_of(j * width, width), width)
                    a_ref[dest, cols] = a_ref[dest, cols] - mm(side, a_ref[rows, cols], TN)
                    return carry

                lax.fori_loop(i, B // width, update, 0)
                a_ref[dest, B : B + TILE] = a_ref[dest, B : B + TILE] - mm(side, a_ref[rows, B : B + TILE], TN)
                return carry

            lax.fori_loop(big + 1, B // width, update_rows, 0)

        return carry

    lax.fori_loop(0, nb, step, 0)

    for k in range(nb):
        cols = slice(k * TILE, (k + 1) * TILE)
        r = lax.broadcasted_iota(jnp.int32, (share, TILE), 0) + col * share
        c = lax.broadcasted_iota(jnp.int32, (share, TILE), 1) + k * TILE
        b_ref[0:share, cols] = jnp.where(r == c, 1.0, 0.0).astype(jnp.float32)
        b_ref[share : 2 * share, cols] = a_ref[cols, B : B + TILE].T[0:share, :]
    for k in range(nb - 1, -1, -1):
        cols = slice(k * TILE, (k + 1) * TILE)
        z = mm(b_ref[:, cols], g_ref[k], NN)
        z_ref[:, cols] = z
        if k > 0:
            b_ref[:, 0 : k * TILE] = b_ref[:, 0 : k * TILE] - mm(z, a_ref[0 : k * TILE, cols], NT)

    own = pl.ds(pl.multiple_of(col * share, share), share)
    to = pl.multiple_of(row * TILE, TILE)
    tile = a_ref[own, pl.ds(to, TILE)]
    r = lax.broadcasted_iota(jnp.int32, (share, TILE), 0) + col * share
    c = lax.broadcasted_iota(jnp.int32, (share, TILE), 1) + to
    diag_ref[...] = jnp.where(c >= r, tile, 0.0).T


def rows_kernel(z_ref, left_ref, rows_ref, weight_ref, panel_ref, update_ref):
    share = panel_ref.shape[0]
    rows = rows_ref[...]
    sq = jnp.sum(rows * rows * weight_ref[...], axis=0, keepdims=True)
    kernel = jnp.exp(dot16(left_ref[...], right_terms(rows, sq, 0), NN))
    both = mm(z_ref[...], kernel[0:B], NN)
    panel_ref[...] = both[0:share]
    update_ref[...] = kernel[B : B + share] - both[share : 2 * share]


def pack(points):
    rows = points.T
    return jnp.concatenate([rows[0:16], rows[16:32]], axis=1)


def local(where, panel, look, scales, row_points):
    share = 2 * look.shape[0]
    rows_dev = row_points.shape[1]
    scales_row = scales.reshape(1, F)
    scales_col = scales.reshape(F, 1)
    vmem = pl.BlockSpec(memory_space=pltpu.VMEM)
    diag, z, left = pl.pallas_call(
        factor_kernel,
        out_shape=(
            jax.ShapeDtypeStruct((B // 8, share), jnp.float32),
            jax.ShapeDtypeStruct((2 * share, B), jnp.float32),
            jax.ShapeDtypeStruct((B + share, 4 * TILE), jnp.bfloat16),
        ),
        in_specs=[pl.BlockSpec(memory_space=pltpu.SMEM), vmem, vmem, vmem, vmem],
        out_specs=(vmem, vmem, vmem),
        scratch_shapes=[
            pltpu.VMEM((B, B + TILE), jnp.float32),
            pltpu.VMEM((B // TILE, TILE, TILE), jnp.float32),
            pltpu.VMEM((2 * share, B), jnp.float32),
            pltpu.VMEM((B + TILE, 4 * TILE), jnp.bfloat16),
        ],
        name="factor",
    )(where, panel, look, scales_row, jnp.zeros(REG, jnp.float32))
    tile = 256
    fixed = lambda shape: pl.BlockSpec(shape, lambda j: (0, 0))
    cols = lambda n: pl.BlockSpec((n, tile), lambda j: (0, j))
    panel_tile, updated = pl.pallas_call(
        rows_kernel,
        grid=(rows_dev // tile,),
        out_shape=(
            jax.ShapeDtypeStruct((share, rows_dev), jnp.float32),
            jax.ShapeDtypeStruct((share, rows_dev), jnp.float32),
        ),
        in_specs=[fixed((2 * share, B)), fixed((B + share, 4 * TILE)), cols(F), fixed((F, 1))],
        out_specs=(cols(share), cols(share)),
        name="rows",
    )(z, left, row_points, scales_col)
    return (diag, panel_tile, updated)


def body(row_points, panel_points, scales):
    n_col = lax.axis_size("col")
    n_row = lax.axis_size("row")
    col = lax.axis_index("col")
    row = lax.axis_index("row")
    share = B // n_col
    rows_dev = row_points.shape[1]
    first = col * share
    look = pack(lax.dynamic_slice_in_dim(row_points, first % rows_dev, share, 1))
    look_all = lax.all_to_all(jnp.broadcast_to(look, (n_row,) + look.shape), "row", 0, 0, tiled=True)
    look = lax.dynamic_index_in_dim(look_all, first // rows_dev, 0, keepdims=False)
    own = pack(panel_points)
    panel = lax.all_to_all(jnp.broadcast_to(own, (n_col,) + own.shape), "col", 0, 0, tiled=True)
    panel = panel.reshape(B // 2, 2 * F)
    where = jnp.stack([col, row]).astype(jnp.int32)
    return local(where, panel, look, scales, row_points)


def solution(mesh):
    return jax.shard_map(
        body,
        mesh=mesh,
        in_specs=(P(None, "row"), P(None, "col"), P()),
        out_specs=(P("row", "col"), P("col", "row"), P("col", "row")),
        check_vma=False,
    )
```

```python
import functools

import jax
import jax.numpy as jnp
from jax import lax
from jax.experimental import pallas as pl
from jax.experimental.pallas import tpu as pltpu
from jax.sharding import PartitionSpec as P

B = 1024
F = 64
RIDGE = 0.5
TILE = 128
REG = (8, 128)
NN = ((1,), (0,))
TN = ((0,), (0,))
NT = ((1,), (1,))


def mm(a, b, dims):
    return lax.dot_general(
        a, b, (dims, ((), ())), precision=lax.Precision.HIGHEST, preferred_element_type=jnp.float32
    )


def row_all(x, i):
    return jnp.broadcast_to(x[i : i + 1, :], REG)


def col_all(x, j):
    return jnp.broadcast_to(x[:, j : j + 1], REG)


def tree_sum(xs):
    xs=list(xs)
    while len(xs)>1:
        xs=[xs[i]+xs[i+1] if i+1<len(xs) else xs[i] for i in range(0,len(xs),2)]
    return xs[0]

def small_chol(d):
    d=[list(x) for x in d]
    rs=[None]*8; l=[[None]*8 for _ in range(8)]
    for s in range(8):
        rs[s]=lax.rsqrt(d[s][s])
        for k in range(s+1,8): l[k][s]=d[k][s]*rs[s]
        for k in range(s+1,8):
            for m in range(s+1,k+1):
                d[k][m]=d[k][m]-l[k][s]*l[m][s]
    return rs,l
def forward(x,rs,l):
    x=list(x)
    for s in range(8):
        x[s]=x[s]*rs[s]
        for k in range(s+1,8): x[k]=x[k]-l[k][s]*x[s]
    return x
def backward(x,rs,l):
    x=list(x)
    for s in range(7,-1,-1):
        x[s]=x[s]*rs[s]
        for k in range(s): x[k]=x[k]-l[s][k]*x[s]
    return x

def factor_tile(W, zero):
    n=len(W); W=list(W)
    sub=lax.broadcasted_iota(jnp.int32,REG,0); lane=lax.broadcasted_iota(jnp.int32,REG,1)
    G=[None]*n
    def entries(cols): return [[row_all(cols[k],i) if i>=k else None for k in range(8)] for i in range(8)]
    def finish(p, rs, l):
        mine=lax.shift_right_logical(lane,3)==p
        w=jnp.where(mine, jnp.where(lane-8*p==sub,1.0,0.0).astype(jnp.float32), W[p])
        w=forward([row_all(w,s) for s in range(8)],rs,l)
        g=w[7]
        for s in range(6,-1,-1): g=jnp.where(sub==s,w[s],g)
        G[p]=jnp.where(lane<8*(p+1),g,0.0)
        return mine,w
    for t in range(n//2):
        p0,p1=2*t,2*t+1
        c0={q:[col_all(W[q],8*p0+k) for k in range(8)] for q in range(p0,n)}
        d1=[col_all(W[p1],8*p1+k) for k in range(8)]
        rs,l=small_chol(entries([x+zero for x in c0[p0]]))
        x=forward(c0[p1],rs,l)
        d1=[d1[k]-tree_sum([x[s]*row_all(x[s],k) for s in range(8)]) for k in range(8)]
        mine,w=finish(p0,rs,l)
        W[p1]=jnp.where(mine,0.0,W[p1])-tree_sum([x[s]*w[s] for s in range(8)])
        v=backward(w,rs,l)
        for q in range(p1+1,n):
            W[q]=jnp.where(mine,0.0,W[q])-tree_sum([c0[q][s]*v[s] for s in range(8)])
        rs,l=small_chol(entries(d1))
        c1={q:[col_all(W[q],8*p1+k) for k in range(8)] for q in range(p1+1,n)}
        mine,w=finish(p1,rs,l)
        v=backward(w,rs,l)
        for q in range(p1+1,n):
            W[q]=jnp.where(mine,0.0,W[q])-tree_sum([c1[q][s]*v[s] for s in range(8)])
    return G

def unpack_points(packed):
    n = packed.shape[0] // 16
    halves = packed.reshape(n, 16, 2 * F)
    return jnp.concatenate([halves[:, :, :F], halves[:, :, F:]], axis=1).reshape(32 * n, F)


def split(x):
    high = x.astype(jnp.bfloat16)
    rest = x - high.astype(jnp.float32)
    middle = rest.astype(jnp.bfloat16)
    low = (rest - middle.astype(jnp.float32)).astype(jnp.bfloat16)
    return high, middle, low


def spread_terms(parts, order, values, axis):
    shape = list(parts[0].shape)
    shape[axis] = TILE
    place = lax.broadcasted_iota(jnp.int32, shape, axis)
    tail = jnp.zeros(shape, jnp.float32)
    for i, v in enumerate(values):
        tail = jnp.where(place == i, v, tail)
    return jnp.concatenate([parts[i] for i in order] + [tail.astype(jnp.bfloat16)], axis=axis)


def as_float(parts):
    return [p.astype(jnp.float32) for p in parts]


LEFT = (0, 0, 1, 0, 1, 2)
RIGHT = (0, 1, 0, 2, 1, 0)


def left_terms(points, scales):
    weighted = points * scales
    sq = jnp.sum(weighted * points, axis=1, keepdims=True)
    return spread_terms(split(2.0 * weighted), LEFT, as_float(split(-sq)) + [1.0, 1.0, 1.0], 1)


def right_terms(points, sq, axis):
    return spread_terms(split(points), RIGHT, [1.0, 1.0, 1.0] + as_float(split(-sq)), axis)


def dot16(a, b, dims):
    return lax.dot_general(a, b, (dims, ((), ())), preferred_element_type=jnp.float32)


def panel_kernel(
    where_ref, pan_ref, look_ref, scales_ref, zero_ref, rows_ref, weight_ref,
    diag_ref, panel_ref, update_ref,
    z_ref, left_ref, a_ref, g_ref, b_ref, right_ref, kern_ref,
):
    nb = B // TILE
    col, row = where_ref[0], where_ref[1]
    scales = scales_ref[...]
    points = unpack_points(pan_ref[...])
    look = unpack_points(look_ref[...])
    share = look.shape[0]
    left_ref[0:B] = left_terms(points, scales)
    left_ref[B : B + share] = left_terms(look, scales)
    others = jnp.concatenate([points, look, jnp.zeros((TILE - share, F), jnp.float32)], axis=0)
    right_ref[...] = right_terms(others, jnp.sum(others * others * scales, axis=1, keepdims=True), 1)
    for i in range(nb):
        at = slice(i * TILE, (i + 1) * TILE)
        block = jnp.exp(dot16(left_ref[at], right_ref[i * TILE :], NT))
        a_ref[at, i * TILE :] = block
        rid = lax.broadcasted_iota(jnp.int32, (TILE, TILE), 0)
        cid = lax.broadcasted_iota(jnp.int32, (TILE, TILE), 1)
        a_ref[at, at] = jnp.where(rid == cid, block[:, 0:TILE] + RIDGE, block[:, 0:TILE])
        if i % 2 == 1:
            a_ref[at, (i - 1) * TILE : i * TILE] = jnp.zeros((TILE, TILE), jnp.float32)

    wide = rows_ref.shape[1] // nb

    def after_tile(k):
        here = slice(k * TILE, (k + 1) * TILE)
        a_ref[here, k * TILE :] = mm(g_ref[k], a_ref[here, k * TILE :], NN)
        if k % 2 == 0:
            later = slice((k + 1) * TILE, (k + 2) * TILE)
            a_ref[later, later.start :] -= mm(a_ref[here, later], a_ref[here, later.start :], TN)
        else:
            pair = slice((k - 1) * TILE, (k + 1) * TILE)
            for i in range(k + 1, nb, 2):
                later = slice(i * TILE, (i + 2) * TILE)
                a_ref[later, i * TILE :] -= mm(a_ref[pair, later], a_ref[pair, i * TILE :], TN)

    def step(k, carry):
        at = pl.multiple_of(k * TILE, TILE)
        G = factor_tile([a_ref[pl.ds(at + 8 * q, 8), pl.ds(at, TILE)] for q in range(TILE // 8)], zero_ref[...])
        for q in range(TILE // 8):
            g_ref[k, 8 * q : 8 * q + 8, :] = G[q]
        to = pl.ds(pl.multiple_of(k * wide, wide), wide)
        rows = rows_ref[:, to]
        sq = jnp.sum(rows * rows * weight_ref[...], axis=0, keepdims=True)
        kern_ref[:, to] = jnp.exp(dot16(left_ref[...], right_terms(rows, sq, 0), NN))
        lax.switch(k, [functools.partial(after_tile, i) for i in range(nb)])
        return carry

    lax.fori_loop(0, nb, step, 0)

    for k in range(nb):
        cols = slice(k * TILE, (k + 1) * TILE)
        r = lax.broadcasted_iota(jnp.int32, (share, TILE), 0) + col * share
        c = lax.broadcasted_iota(jnp.int32, (share, TILE), 1) + k * TILE
        b_ref[0:share, cols] = jnp.where(r == c, 1.0, 0.0).astype(jnp.float32)
        b_ref[share : 2 * share, cols] = a_ref[cols, B : B + TILE].T[0:share, :]
    for k in range(nb - 1, -1, -1):
        cols = slice(k * TILE, (k + 1) * TILE)
        z = mm(b_ref[:, cols], g_ref[k], NN)
        z_ref[:, cols] = z
        if k > 0:
            b_ref[:, 0 : k * TILE] = b_ref[:, 0 : k * TILE] - mm(z, a_ref[0 : k * TILE, cols], NT)

    own = pl.ds(pl.multiple_of(col * share, share), share)
    to = pl.multiple_of(row * TILE, TILE)
    tile = a_ref[own, pl.ds(to, TILE)]
    r = lax.broadcasted_iota(jnp.int32, (share, TILE), 0) + col * share
    c = lax.broadcasted_iota(jnp.int32, (share, TILE), 1) + to
    diag_ref[...] = jnp.where(c >= r, tile, 0.0)

    block = 2 * wide

    def product(j, carry):
        to = pl.ds(pl.multiple_of(j * block, block), block)
        both = mm(z_ref[...], kern_ref[0:B, to], NN)
        panel_ref[:, to] = both[0:share]
        update_ref[:, to] = kern_ref[B : B + share, to] - both[share : 2 * share]
        return carry

    lax.fori_loop(0, rows_ref.shape[1] // block, product, 0)


def pack(points):
    rows = points.T
    return jnp.concatenate([rows[0:16], rows[16:32]], axis=1)


def local(where, panel, look, scales, row_points):
    share = 2 * look.shape[0]
    rows_dev = row_points.shape[1]
    scales_row = scales.reshape(1, F)
    scales_col = scales.reshape(F, 1)
    vmem = pl.BlockSpec(memory_space=pltpu.VMEM)
    out = jax.ShapeDtypeStruct((share, rows_dev), jnp.float32)
    diag, panel_tile, updated = pl.pallas_call(
        panel_kernel,
        out_shape=(jax.ShapeDtypeStruct((share, B // 8), jnp.float32), out, out),
        in_specs=[pl.BlockSpec(memory_space=pltpu.SMEM)] + [vmem] * 6,
        out_specs=(vmem, vmem, vmem),
        scratch_shapes=[
            pltpu.VMEM((2 * share, B), jnp.float32),
            pltpu.VMEM((B + share, 4 * TILE), jnp.bfloat16),
            pltpu.VMEM((B, B + TILE), jnp.float32),
            pltpu.VMEM((B // TILE, TILE, TILE), jnp.float32),
            pltpu.VMEM((2 * share, B), jnp.float32),
            pltpu.VMEM((B + TILE, 4 * TILE), jnp.bfloat16),
            pltpu.VMEM((B + share, rows_dev), jnp.float32),
        ],
        name="panel",
    )(where, panel, look, scales_row, jnp.zeros(REG, jnp.float32), row_points, scales_col)
    return (diag.T, panel_tile, updated)


def body(row_points, panel_points, scales):
    n_col = lax.axis_size("col")
    n_row = lax.axis_size("row")
    col = lax.axis_index("col")
    row = lax.axis_index("row")
    share = B // n_col
    rows_dev = row_points.shape[1]
    first = col * share
    own = pack(panel_points)
    panel = lax.all_to_all(jnp.broadcast_to(own, (n_col,) + own.shape), "col", 0, 0, tiled=True)
    panel = panel.reshape(B // 2, 2 * F)
    look = pack(lax.dynamic_slice_in_dim(row_points, first % rows_dev, share, 1))
    sent = [lax.ppermute(look, "row", [(0, to)]) for to in range(1, n_row)]
    look = jnp.where(row == 0, look, sum(sent[1:], sent[0]))
    where = jnp.stack([col, row]).astype(jnp.int32)
    return local(where, panel, look, scales, row_points)


def solution(mesh):
    return jax.shard_map(
        body,
        mesh=mesh,
        in_specs=(P(None, "row"), P(None, "col"), P()),
        out_specs=(P("row", "col"), P("col", "row"), P("col", "row")),
        check_vma=False,
    )
```

```python
import functools

import jax
import jax.numpy as jnp
from jax import lax
from jax.experimental import pallas as pl
from jax.experimental.pallas import tpu as pltpu
from jax.sharding import PartitionSpec as P

B = 1024
F = 64
RIDGE = 0.5
TILE = 128
REG = (8, 128)
NEAR = 4
NN = ((1,), (0,))
TN = ((0,), (0,))
NT = ((1,), (1,))


def mm(a, b, dims):
    return lax.dot_general(
        a, b, (dims, ((), ())), precision=lax.Precision.HIGHEST, preferred_element_type=jnp.float32
    )


def row_all(x, i):
    return jnp.broadcast_to(x[i : i + 1, :], REG)


def col_all(x, j):
    return jnp.broadcast_to(x[:, j : j + 1], REG)


def tree_sum(xs):
    xs=list(xs)
    while len(xs)>1:
        xs=[xs[i]+xs[i+1] if i+1<len(xs) else xs[i] for i in range(0,len(xs),2)]
    return xs[0]

def small_chol(d):
    d=[list(x) for x in d]
    rs=[None]*8; l=[[None]*8 for _ in range(8)]
    for s in range(0,8,2):
        a,b,c=d[s][s],d[s+1][s],d[s+1][s+1]
        det=a*c-b*b
        r0=lax.rsqrt(a)
        l10=b*r0
        rd=lax.rsqrt(det)
        inv=rd*rd
        r1=(a*r0)*rd
        r01=r0*rd
        rs[s]=r0; rs[s+1]=r1
        l[s+1][s]=l10
        y0={};y1={}
        for k in range(s+2,8):
            y0[k]=c*d[k][s]-b*d[k][s+1]
            y1[k]=a*d[k][s+1]-b*d[k][s]
            l[k][s]=d[k][s]*r0
            l[k][s+1]=y1[k]*r01
        for k in range(s+2,8):
            for m in range(s+2,k+1):
                d[k][m]=d[k][m]-(y0[k]*d[m][s]+y1[k]*d[m][s+1])*inv
    return rs,l
def forward(x,rs,l):
    x=list(x)
    for s in range(8):
        x[s]=x[s]*rs[s]
        for k in range(s+1,8): x[k]=x[k]-l[k][s]*x[s]
    return x
def backward(x,rs,l):
    x=list(x)
    for s in range(7,-1,-1):
        x[s]=x[s]*rs[s]
        for k in range(s): x[k]=x[k]-l[s][k]*x[s]
    return x

def factor_tile(W, zero):
    n=len(W); W=list(W)
    sub=lax.broadcasted_iota(jnp.int32,REG,0); lane=lax.broadcasted_iota(jnp.int32,REG,1)
    G=[None]*n
    def entries(cols): return [[row_all(cols[k],i) if i>=k else None for k in range(8)] for i in range(8)]
    def finish(p, rs, l):
        mine=lax.shift_right_logical(lane,3)==p
        w=jnp.where(mine, jnp.where(lane-8*p==sub,1.0,0.0).astype(jnp.float32), W[p])
        w=forward([row_all(w,s) for s in range(8)],rs,l)
        g=w[7]
        for s in range(6,-1,-1): g=jnp.where(sub==s,w[s],g)
        G[p]=jnp.where(lane<8*(p+1),g,0.0)
        return mine,w
    for t in range(n//2):
        p0,p1=2*t,2*t+1
        near=range(p1+1,min(p1+1+NEAR,n)); far=range(min(p1+1+NEAR,n),n)
        c0={q:[col_all(W[q],8*p0+k) for k in range(8)] for q in (p0,p1)}
        d1=[col_all(W[p1],8*p1+k) for k in range(8)]
        c0.update({q:[col_all(W[q],8*p0+k) for k in range(8)] for q in near})
        old=list(W)
        rs,l=small_chol(entries([x+zero for x in c0[p0]]))
        x=forward(c0[p1],rs,l)
        d1=[d1[k]-tree_sum([x[s]*row_all(x[s],k) for s in range(8)]) for k in range(8)]
        mine0,w=finish(p0,rs,l)
        W[p1]=jnp.where(mine0,0.0,W[p1])-tree_sum([x[s]*w[s] for s in range(8)])
        v0=backward(w,rs,l)
        for q in near:
            W[q]=jnp.where(mine0,0.0,W[q])-tree_sum([c0[q][s]*v0[s] for s in range(8)])
        rs,l=small_chol(entries(d1))
        c1={q:[col_all(W[q],8*p1+k) for k in range(8)] for q in near}
        mine1,w=finish(p1,rs,l)
        v1=backward(w,rs,l)
        for q in near:
            W[q]=jnp.where(mine1,0.0,W[q])-tree_sum([c1[q][s]*v1[s] for s in range(8)])
        if len(far):
            def pick(v):
                o=v[7]
                for s in range(6,-1,-1): o=jnp.where(sub==s,v[s],o)
                return o
            V0=pick(v0); V1=pick(v1)
            V0=jnp.where(mine1,0.0,V0)-tree_sum([col_all(V0,8*p1+k)*v1[k] for k in range(8)])
            z=jnp.zeros(REG,jnp.float32)
            rhs=jnp.concatenate([z]*p0+[V0,V1]+[z]*(n-p1-1),0)
            prod=lax.dot_general(jnp.concatenate([old[q] for q in far],0),rhs,(((1,),(0,)),((),())),precision=lax.Precision.HIGHEST,preferred_element_type=jnp.float32)
            for i,q in enumerate(far):
                W[q]=jnp.where(mine0|mine1,0.0,W[q])-prod[8*i:8*i+8]
    return G


def unpack_points(packed):
    n = packed.shape[0] // 16
    halves = packed.reshape(n, 16, 2 * F)
    return jnp.concatenate([halves[:, :, :F], halves[:, :, F:]], axis=1).reshape(32 * n, F)


def split(x):
    high = x.astype(jnp.bfloat16)
    rest = x - high.astype(jnp.float32)
    middle = rest.astype(jnp.bfloat16)
    low = (rest - middle.astype(jnp.float32)).astype(jnp.bfloat16)
    return high, middle, low


def stacked(a, b):
    n = a.shape[0]
    high, middle, low = split(a)
    b = split(b)
    first = dot16(jnp.concatenate([high, middle, low], axis=0), b[0], NN)
    second = dot16(jnp.concatenate([high, middle], axis=0), b[1], NN)
    small = first[2 * n :] + second[n:] + dot16(high, b[2], NN)
    return first[0:n] + (first[n : 2 * n] + second[0:n] + small)


def chained(a, b):
    a, b = split(a), split(b)
    left = jnp.concatenate([a[i] for i in (0, 0, 1, 1, 0, 2)], axis=1)
    right = jnp.concatenate([b[i] for i in (0, 1, 0, 1, 2, 0)], axis=0)
    return dot16(left, right, NN)


def spread_terms(parts, order, values, axis):
    shape = list(parts[0].shape)
    shape[axis] = TILE
    place = lax.broadcasted_iota(jnp.int32, shape, axis)
    tail = jnp.zeros(shape, jnp.float32)
    for i, v in enumerate(values):
        tail = jnp.where(place == i, v, tail)
    return jnp.concatenate([parts[i] for i in order] + [tail.astype(jnp.bfloat16)], axis=axis)


def as_float(parts):
    return [p.astype(jnp.float32) for p in parts]


LEFT = (0, 0, 1, 0, 1, 2)
RIGHT = (0, 1, 0, 2, 1, 0)


def left_terms(points, scales):
    weighted = points * scales
    sq = jnp.sum(weighted * points, axis=1, keepdims=True)
    return spread_terms(split(2.0 * weighted), LEFT, as_float(split(-sq)) + [1.0, 1.0, 1.0], 1)


def right_terms(points, sq, axis):
    return spread_terms(split(points), RIGHT, [1.0, 1.0, 1.0] + as_float(split(-sq)), axis)


def dot16(a, b, dims):
    return lax.dot_general(a, b, (dims, ((), ())), preferred_element_type=jnp.float32)


def panel_kernel(
    pan_ref, look_ref, scales_ref, rows_ref,
    diag_ref, panel_ref, update_ref,
    z_ref, left_ref, a_ref, g_ref, b_ref, right_ref, kern_ref, weight_ref,
):
    nb = B // TILE
    col, row = lax.axis_index("col"), lax.axis_index("row")
    scales = scales_ref[...]
    weight_ref[...] = jnp.broadcast_to(jnp.broadcast_to(scales, (8, F)).T[:, 0:1], (F, TILE))
    zero = jnp.full(REG, jnp.minimum(col, 0).astype(jnp.float32))
    points = unpack_points(pan_ref[...])
    look = unpack_points(look_ref[...])
    share = look.shape[0]
    left_ref[0:B] = left_terms(points, scales)
    left_ref[B : B + share] = left_terms(look, scales)
    others = jnp.concatenate([points, look, jnp.zeros((TILE - share, F), jnp.float32)], axis=0)
    right_ref[...] = right_terms(others, jnp.sum(others * others * scales, axis=1, keepdims=True), 1)
    for i in range(nb):
        at = slice(i * TILE, (i + 1) * TILE)
        block = jnp.exp(dot16(left_ref[at], right_ref[i * TILE :], NT))
        a_ref[at, i * TILE :] = block
        rid = lax.broadcasted_iota(jnp.int32, (TILE, TILE), 0)
        cid = lax.broadcasted_iota(jnp.int32, (TILE, TILE), 1)
        a_ref[at, at] = jnp.where(rid == cid, block[:, 0:TILE] + RIDGE, block[:, 0:TILE])
        if i % 2 == 1:
            a_ref[at, (i - 1) * TILE : i * TILE] = jnp.zeros((TILE, TILE), jnp.float32)

    wide = rows_ref.shape[1] // nb

    def after_tile(k):
        here = slice(k * TILE, (k + 1) * TILE)
        a_ref[here, k * TILE :] = chained(g_ref[k], a_ref[here, k * TILE :])
        if k % 2 == 0:
            later = slice((k + 1) * TILE, (k + 2) * TILE)
            a_ref[later, later.start :] -= mm(a_ref[here, later], a_ref[here, later.start :], TN)
        else:
            pair = slice((k - 1) * TILE, (k + 1) * TILE)
            for i in range(k + 1, nb, 2):
                later = slice(i * TILE, (i + 2) * TILE)
                a_ref[later, i * TILE :] -= mm(a_ref[pair, later], a_ref[pair, i * TILE :], TN)

    def step(k, carry):
        at = pl.multiple_of(k * TILE, TILE)
        G = factor_tile([a_ref[pl.ds(at + 8 * q, 8), pl.ds(at, TILE)] for q in range(TILE // 8)], zero)
        for q in range(TILE // 8):
            g_ref[k, 8 * q : 8 * q + 8, :] = G[q]
        to = pl.ds(pl.multiple_of(k * wide, wide), wide)
        rows = rows_ref[:, to]
        sq = jnp.sum(rows * rows * weight_ref[:, 0:1], axis=0, keepdims=True)
        kern_ref[:, to] = jnp.exp(dot16(left_ref[...], right_terms(rows, sq, 0), NN))
        lax.switch(k, [functools.partial(after_tile, i) for i in range(nb)])
        return carry

    lax.fori_loop(0, nb, step, 0)

    for k in range(nb):
        cols = slice(k * TILE, (k + 1) * TILE)
        r = lax.broadcasted_iota(jnp.int32, (share, TILE), 0) + col * share
        c = lax.broadcasted_iota(jnp.int32, (share, TILE), 1) + k * TILE
        b_ref[0:share, cols] = jnp.where(r == c, 1.0, 0.0).astype(jnp.float32)
        b_ref[share : 2 * share, cols] = a_ref[cols, B : B + TILE].T[0:share, :]
    for k in range(nb - 1, -1, -1):
        cols = slice(k * TILE, (k + 1) * TILE)
        z = mm(b_ref[:, cols], g_ref[k], NN)
        z_ref[:, cols] = z
        if k > 0:
            b_ref[:, 0 : k * TILE] = b_ref[:, 0 : k * TILE] - mm(z, a_ref[0 : k * TILE, cols], NT)

    own = pl.ds(pl.multiple_of(col * share, share), share)
    to = pl.multiple_of(row * TILE, TILE)
    tile = a_ref[own, pl.ds(to, TILE)]
    r = lax.broadcasted_iota(jnp.int32, (share, TILE), 0) + col * share
    c = lax.broadcasted_iota(jnp.int32, (share, TILE), 1) + to
    diag_ref[...] = jnp.where(c >= r, tile, 0.0)

    block = 2 * wide

    def product(j, carry):
        to = pl.ds(pl.multiple_of(j * block, block), block)
        both = stacked(z_ref[...], kern_ref[0:B, to])
        panel_ref[:, to] = both[0:share]
        update_ref[:, to] = kern_ref[B : B + share, to] - both[share : 2 * share]
        return carry

    lax.fori_loop(0, rows_ref.shape[1] // block, product, 0)


def pack(points, copies):
    rows = jnp.broadcast_to(points.T, (copies,) + points.shape[::-1])
    return jnp.concatenate([rows[:, 0:16], rows[:, 16:32]], axis=2)


def local(panel, look, scales, row_points):
    share = 2 * look.shape[0]
    rows_dev = row_points.shape[1]
    vmem = pl.BlockSpec(memory_space=pltpu.VMEM)
    out = jax.ShapeDtypeStruct((share, rows_dev), jnp.float32)
    diag, panel_tile, updated = pl.pallas_call(
        panel_kernel,
        out_shape=(jax.ShapeDtypeStruct((share, B // 8), jnp.float32), out, out),
        in_specs=[vmem] * 4,
        out_specs=(vmem, vmem, vmem),
        scratch_shapes=[
            pltpu.VMEM((2 * share, B), jnp.float32),
            pltpu.VMEM((B + share, 4 * TILE), jnp.bfloat16),
            pltpu.VMEM((B, B + TILE), jnp.float32),
            pltpu.VMEM((B // TILE, TILE, TILE), jnp.float32),
            pltpu.VMEM((2 * share, B), jnp.float32),
            pltpu.VMEM((B + TILE, 4 * TILE), jnp.bfloat16),
            pltpu.VMEM((B + share, rows_dev), jnp.float32),
            pltpu.VMEM((F, TILE), jnp.float32),
        ],
        name="panel",
    )(panel, look, scales.reshape(1, F), row_points)
    return (diag.T, panel_tile, updated)


def body(row_points, panel_points, scales):
    n_col = lax.axis_size("col")
    n_row = lax.axis_size("row")
    col = lax.axis_index("col")
    row = lax.axis_index("row")
    share = B // n_col
    rows_dev = row_points.shape[1]
    first = col * share
    panel = lax.all_to_all(pack(panel_points, n_col), "col", 0, 0, tiled=True)
    panel = panel.reshape(B // 2, 2 * F)
    look = pack(lax.dynamic_slice_in_dim(row_points, first % rows_dev, share, 1), 1)[0]
    sent = [lax.ppermute(look, "row", [(0, to)]) for to in range(1, n_row)]
    look = jnp.where(row == 0, look, sum(sent[1:], sent[0]))
    return local(panel, look, scales, row_points)


def solution(mesh):
    return jax.shard_map(
        body,
        mesh=mesh,
        in_specs=(P(None, "row"), P(None, "col"), P()),
        out_specs=(P("row", "col"), P("col", "row"), P("col", "row")),
        check_vma=False,
    )
```

```python
import functools

import jax
import jax.numpy as jnp
from jax import lax
from jax.experimental import pallas as pl
from jax.experimental.pallas import tpu as pltpu
from jax.sharding import PartitionSpec as P

B = 1024
F = 64
RIDGE = 0.5
TILE = 128
REG = (8, 128)
NEAR = 4
NN = ((1,), (0,))
TN = ((0,), (0,))
NT = ((1,), (1,))


def mm(a, b, dims):
    return lax.dot_general(
        a, b, (dims, ((), ())), precision=lax.Precision.HIGHEST, preferred_element_type=jnp.float32
    )


def row_all(x, i):
    return jnp.broadcast_to(x[i : i + 1, :], REG)


def col_all(x, j):
    return jnp.broadcast_to(x[:, j : j + 1], REG)


def tree_sum(xs):
    xs=list(xs)
    while len(xs)>1:
        xs=[xs[i]+xs[i+1] if i+1<len(xs) else xs[i] for i in range(0,len(xs),2)]
    return xs[0]

def small_chol(d):
    d=list(d)
    rs=[None]*8; l=[[None]*8 for _ in range(8)]
    for s in range(0,8,2):
        a,b,c=row_all(d[s],s),row_all(d[s],s+1),row_all(d[s+1],s+1)
        det=a*c-b*b
        r0=lax.rsqrt(a); rd=lax.rsqrt(det); inv=rd*rd
        rs[s]=r0; rs[s+1]=(a*r0)*rd
        y1=a*d[s+1]-b*d[s]
        l0=d[s]*r0; l1=y1*(r0*rd)
        for k in range(s+1,8): l[k][s]=row_all(l0,k)
        for k in range(s+2,8): l[k][s+1]=row_all(l1,k)
        if s<6:
            y0=c*d[s]-b*d[s+1]
            for m in range(s+2,8):
                d[m]=d[m]-(y0*row_all(d[s],m)+y1*row_all(d[s+1],m))*inv
    return rs,l
def forward(x,rs,l):
    x=list(x)
    for s in range(8):
        x[s]=x[s]*rs[s]
        for k in range(s+1,8): x[k]=x[k]-l[k][s]*x[s]
    return x
def backward(x,rs,l):
    x=list(x)
    for s in range(7,-1,-1):
        x[s]=x[s]*rs[s]
        for k in range(s): x[k]=x[k]-l[s][k]*x[s]
    return x

def factor_tile(W, zero):
    n=len(W); W=list(W)
    sub=lax.broadcasted_iota(jnp.int32,REG,0); lane=lax.broadcasted_iota(jnp.int32,REG,1)
    G=[None]*n
    def finish(p, rs, l):
        mine=lax.shift_right_logical(lane,3)==p
        w=jnp.where(mine, jnp.where(lane-8*p==sub,1.0,0.0).astype(jnp.float32), W[p])
        w=forward([row_all(w,s) for s in range(8)],rs,l)
        g=w[7]
        for s in range(6,-1,-1): g=jnp.where(sub==s,w[s],g)
        G[p]=jnp.where(lane<8*(p+1),g,0.0)
        return mine,w
    for t in range(n//2):
        p0,p1=2*t,2*t+1
        near=range(p1+1,min(p1+1+NEAR,n)); far=range(min(p1+1+NEAR,n),n)
        c0={q:[col_all(W[q],8*p0+k) for k in range(8)] for q in (p0,p1)}
        d1=[col_all(W[p1],8*p1+k) for k in range(8)]
        c0.update({q:[col_all(W[q],8*p0+k) for k in range(8)] for q in near})
        old=list(W)
        rs,l=small_chol([x+zero for x in c0[p0]])
        x=forward(c0[p1],rs,l)
        d1=[d1[k]-tree_sum([x[s]*row_all(x[s],k) for s in range(8)]) for k in range(8)]
        mine0,w=finish(p0,rs,l)
        W[p1]=jnp.where(mine0,0.0,W[p1])-tree_sum([x[s]*w[s] for s in range(8)])
        v0=backward(w,rs,l)
        for q in near:
            W[q]=jnp.where(mine0,0.0,W[q])-tree_sum([c0[q][s]*v0[s] for s in range(8)])
        rs,l=small_chol(d1)
        c1={q:[col_all(W[q],8*p1+k) for k in range(8)] for q in near}
        mine1,w=finish(p1,rs,l)
        v1=backward(w,rs,l)
        for q in near:
            W[q]=jnp.where(mine1,0.0,W[q])-tree_sum([c1[q][s]*v1[s] for s in range(8)])
        if len(far):
            def pick(v):
                o=v[7]
                for s in range(6,-1,-1): o=jnp.where(sub==s,v[s],o)
                return o
            V0=pick(v0); V1=pick(v1)
            V0=jnp.where(mine1,0.0,V0)-tree_sum([col_all(V0,8*p1+k)*v1[k] for k in range(8)])
            z=jnp.zeros(REG,jnp.float32)
            rhs=jnp.concatenate([z]*p0+[V0,V1]+[z]*(n-p1-1),0)
            prod=lax.dot_general(jnp.concatenate([old[q] for q in far],0),rhs,(((1,),(0,)),((),())),precision=lax.Precision.HIGHEST,preferred_element_type=jnp.float32)
            for i,q in enumerate(far):
                W[q]=jnp.where(mine0|mine1,0.0,W[q])-prod[8*i:8*i+8]
    return G


def unpack_points(packed):
    n = packed.shape[0] // 16
    halves = packed.reshape(n, 16, 2 * F)
    return jnp.concatenate([halves[:, :, :F], halves[:, :, F:]], axis=1).reshape(32 * n, F)


def split(x):
    high = x.astype(jnp.bfloat16)
    rest = x - high.astype(jnp.float32)
    middle = rest.astype(jnp.bfloat16)
    low = (rest - middle.astype(jnp.float32)).astype(jnp.bfloat16)
    return high, middle, low


def stacked(a, b, dims=NN):
    n = a.shape[0]
    high, middle, low = split(a)
    b = split(b)
    first = dot16(jnp.concatenate([high, middle, low], axis=0), b[0], dims)
    second = dot16(jnp.concatenate([high, middle], axis=0), b[1], dims)
    small = first[2 * n :] + second[n:] + dot16(high, b[2], dims)
    return first[0:n] + (first[n : 2 * n] + second[0:n] + small)


def chained(a, b):
    a, b = split(a), split(b)
    left = jnp.concatenate([a[i] for i in (0, 0, 1, 1, 0, 2)], axis=1)
    right = jnp.concatenate([b[i] for i in (0, 1, 0, 1, 2, 0)], axis=0)
    return dot16(left, right, NN)


def spread_terms(parts, order, values, axis):
    shape = list(parts[0].shape)
    shape[axis] = TILE
    place = lax.broadcasted_iota(jnp.int32, shape, axis)
    tail = jnp.zeros(shape, jnp.float32)
    for i, v in enumerate(values):
        tail = jnp.where(place == i, v, tail)
    return jnp.concatenate([parts[i] for i in order] + [tail.astype(jnp.bfloat16)], axis=axis)


def as_float(parts):
    return [p.astype(jnp.float32) for p in parts]


LEFT = (0, 0, 1, 0, 1, 2)
RIGHT = (0, 1, 0, 2, 1, 0)


def left_terms(points, scales):
    weighted = points * scales
    sq = jnp.sum(weighted * points, axis=1, keepdims=True)
    return spread_terms(split(2.0 * weighted), LEFT, as_float(split(-sq)) + [1.0, 1.0, 1.0], 1)


def right_terms(points, sq, axis):
    return spread_terms(split(points), RIGHT, [1.0, 1.0, 1.0] + as_float(split(-sq)), axis)


def dot16(a, b, dims):
    return lax.dot_general(a, b, (dims, ((), ())), preferred_element_type=jnp.float32)


def panel_kernel(
    pan_ref, look_ref, scales_ref, rows_ref,
    diag_ref, panel_ref, update_ref,
    z_ref, left_ref, a_ref, g_ref, b_ref, right_ref, kern_ref, weight_ref,
):
    nb = B // TILE
    col, row = lax.axis_index("col"), lax.axis_index("row")
    scales = scales_ref[...]
    weight_ref[...] = jnp.broadcast_to(jnp.broadcast_to(scales, (8, F)).T[:, 0:1], (F, TILE))
    zero = jnp.full(REG, jnp.minimum(col, 0).astype(jnp.float32))
    points = unpack_points(pan_ref[...])
    look = unpack_points(look_ref[...])
    share = look.shape[0]
    left_ref[0:B] = left_terms(points, scales)
    left_ref[B : B + share] = left_terms(look, scales)
    others = jnp.concatenate([points, look, jnp.zeros((TILE - share, F), jnp.float32)], axis=0)
    right_ref[...] = right_terms(others, jnp.sum(others * others * scales, axis=1, keepdims=True), 1)
    for i in range(nb):
        at = slice(i * TILE, (i + 1) * TILE)
        block = jnp.exp(dot16(left_ref[at], right_ref[i * TILE :], NT))
        a_ref[at, i * TILE :] = block
        rid = lax.broadcasted_iota(jnp.int32, (TILE, TILE), 0)
        cid = lax.broadcasted_iota(jnp.int32, (TILE, TILE), 1)
        a_ref[at, at] = jnp.where(rid == cid, block[:, 0:TILE] + RIDGE, block[:, 0:TILE])
        if i % 2 == 1:
            a_ref[at, (i - 1) * TILE : i * TILE] = jnp.zeros((TILE, TILE), jnp.float32)

    wide = rows_ref.shape[1] // nb

    def after_tile(k):
        here = slice(k * TILE, (k + 1) * TILE)
        a_ref[here, k * TILE :] = chained(g_ref[k], a_ref[here, k * TILE :])
        if k % 2 == 0:
            later = slice((k + 1) * TILE, (k + 2) * TILE)
            a_ref[later, later.start :] -= mm(a_ref[here, later], a_ref[here, later.start :], TN)
        else:
            pair = slice((k - 1) * TILE, (k + 1) * TILE)
            for i in range(k + 1, nb, 2):
                later = slice(i * TILE, (i + 2) * TILE)
                a_ref[later, i * TILE :] -= mm(a_ref[pair, later], a_ref[pair, i * TILE :], TN)

    def step(k, carry):
        at = pl.multiple_of(k * TILE, TILE)
        G = factor_tile([a_ref[pl.ds(at + 8 * q, 8), pl.ds(at, TILE)] for q in range(TILE // 8)], zero)
        for q in range(TILE // 8):
            g_ref[k, 8 * q : 8 * q + 8, :] = G[q]
        to = pl.ds(pl.multiple_of(k * wide, wide), wide)
        rows = rows_ref[:, to]
        sq = jnp.sum(rows * rows * weight_ref[:, 0:1], axis=0, keepdims=True)
        kern_ref[:, to] = jnp.exp(dot16(left_ref[...], right_terms(rows, sq, 0), NN))
        lax.switch(k, [functools.partial(after_tile, i) for i in range(nb)])
        return carry

    lax.fori_loop(0, nb, step, 0)

    for k in range(nb):
        cols = slice(k * TILE, (k + 1) * TILE)
        r = lax.broadcasted_iota(jnp.int32, (share, TILE), 0) + col * share
        c = lax.broadcasted_iota(jnp.int32, (share, TILE), 1) + k * TILE
        b_ref[0:share, cols] = jnp.where(r == c, 1.0, 0.0).astype(jnp.float32)
        b_ref[share : 2 * share, cols] = a_ref[cols, B : B + TILE].T[0:share, :]
    for k in range(nb - 1, -1, -1):
        cols = slice(k * TILE, (k + 1) * TILE)
        z = stacked(b_ref[:, cols], g_ref[k])
        z_ref[:, cols] = z
        if k > 0:
            b_ref[:, 0 : k * TILE] = b_ref[:, 0 : k * TILE] - stacked(z, a_ref[0 : k * TILE, cols], NT)

    own = pl.ds(pl.multiple_of(col * share, share), share)
    to = pl.multiple_of(row * TILE, TILE)
    tile = a_ref[own, pl.ds(to, TILE)]
    r = lax.broadcasted_iota(jnp.int32, (share, TILE), 0) + col * share
    c = lax.broadcasted_iota(jnp.int32, (share, TILE), 1) + to
    diag_ref[...] = jnp.where(c >= r, tile, 0.0)

    block = 2 * wide

    def product(j, carry):
        to = pl.ds(pl.multiple_of(j * block, block), block)
        both = stacked(z_ref[...], kern_ref[0:B, to])
        panel_ref[:, to] = both[0:share]
        update_ref[:, to] = kern_ref[B : B + share, to] - both[share : 2 * share]
        return carry

    lax.fori_loop(0, rows_ref.shape[1] // block, product, 0)


def pack(points, copies):
    rows = jnp.broadcast_to(points.T, (copies,) + points.shape[::-1])
    return jnp.concatenate([rows[:, 0:16], rows[:, 16:32]], axis=2)


def local(panel, look, scales, row_points):
    share = 2 * look.shape[0]
    rows_dev = row_points.shape[1]
    vmem = pl.BlockSpec(memory_space=pltpu.VMEM)
    out = jax.ShapeDtypeStruct((share, rows_dev), jnp.float32)
    diag, panel_tile, updated = pl.pallas_call(
        panel_kernel,
        out_shape=(jax.ShapeDtypeStruct((share, B // 8), jnp.float32), out, out),
        in_specs=[vmem] * 4,
        out_specs=(vmem, vmem, vmem),
        scratch_shapes=[
            pltpu.VMEM((2 * share, B), jnp.float32),
            pltpu.VMEM((B + share, 4 * TILE), jnp.bfloat16),
            pltpu.VMEM((B, B + TILE), jnp.float32),
            pltpu.VMEM((B // TILE, TILE, TILE), jnp.float32),
            pltpu.VMEM((2 * share, B), jnp.float32),
            pltpu.VMEM((B + TILE, 4 * TILE), jnp.bfloat16),
            pltpu.VMEM((B + share, rows_dev), jnp.float32),
            pltpu.VMEM((F, TILE), jnp.float32),
        ],
        name="panel",
    )(panel, look, scales.reshape(1, F), row_points)
    return (diag.T, panel_tile, updated)


def body(row_points, panel_points, scales):
    n_col = lax.axis_size("col")
    n_row = lax.axis_size("row")
    col = lax.axis_index("col")
    row = lax.axis_index("row")
    share = B // n_col
    rows_dev = row_points.shape[1]
    first = col * share
    panel = lax.all_to_all(pack(panel_points, n_col), "col", 0, 0, tiled=True)
    panel = panel.reshape(B // 2, 2 * F)
    look = pack(lax.dynamic_slice_in_dim(row_points, first % rows_dev, share, 1), 1)[0]
    sent = [lax.ppermute(look, "row", [(0, to)]) for to in range(1, n_row)]
    look = jnp.where(row == 0, look, sum(sent[1:], sent[0]))
    return local(panel, look, scales, row_points)


def solution(mesh):
    return jax.shard_map(
        body,
        mesh=mesh,
        in_specs=(P(None, "row"), P(None, "col"), P()),
        out_specs=(P("row", "col"), P("col", "row"), P("col", "row")),
        check_vma=False,
    )
```

```python
import functools

import jax
import jax.numpy as jnp
from jax import lax
from jax.experimental import pallas as pl
from jax.experimental.pallas import tpu as pltpu
from jax.sharding import PartitionSpec as P

B = 1024
F = 64
RIDGE = 0.5
TILE = 128
REG = (8, 128)
NEAR = 4
NN = ((1,), (0,))
TN = ((0,), (0,))
NT = ((1,), (1,))


def mm(a, b, dims):
    return lax.dot_general(
        a, b, (dims, ((), ())), precision=lax.Precision.HIGHEST, preferred_element_type=jnp.float32
    )


def row_all(x, i):
    return jnp.broadcast_to(x[i : i + 1, :], REG)


def col_all(x, j):
    return jnp.broadcast_to(x[:, j : j + 1], REG)


def tree_sum(xs):
    xs=list(xs)
    while len(xs)>1:
        xs=[xs[i]+xs[i+1] if i+1<len(xs) else xs[i] for i in range(0,len(xs),2)]
    return xs[0]

def small_chol(d):
    d=list(d)
    rs=[None]*8; l=[[None]*8 for _ in range(8)]
    for s in range(0,8,2):
        a,b,c=row_all(d[s],s),row_all(d[s],s+1),row_all(d[s+1],s+1)
        det=a*c-b*b
        r0=lax.rsqrt(a); rd=lax.rsqrt(det); inv=rd*rd
        rs[s]=r0; rs[s+1]=(a*r0)*rd
        y1=a*d[s+1]-b*d[s]
        l0=d[s]*r0; l1=y1*(r0*rd)
        for k in range(s+1,8): l[k][s]=row_all(l0,k)
        for k in range(s+2,8): l[k][s+1]=row_all(l1,k)
        if s<6:
            y0=c*d[s]-b*d[s+1]
            for m in range(s+2,8):
                d[m]=d[m]-(y0*row_all(d[s],m)+y1*row_all(d[s+1],m))*inv
    return rs,l
def forward(x,rs,l):
    x=list(x)
    for s in range(8):
        x[s]=x[s]*rs[s]
        for k in range(s+1,8): x[k]=x[k]-l[k][s]*x[s]
    return x
def backward(x,rs,l):
    x=list(x)
    for s in range(7,-1,-1):
        x[s]=x[s]*rs[s]
        for k in range(s): x[k]=x[k]-l[s][k]*x[s]
    return x

def factor_tile(W, zero):
    n=len(W); W=list(W)
    sub=lax.broadcasted_iota(jnp.int32,REG,0); lane=lax.broadcasted_iota(jnp.int32,REG,1)
    G=[None]*n
    def finish(p, rs, l):
        mine=lax.shift_right_logical(lane,3)==p
        w=jnp.where(mine, jnp.where(lane-8*p==sub,1.0,0.0).astype(jnp.float32), W[p])
        w=forward([row_all(w,s) for s in range(8)],rs,l)
        g=w[7]
        for s in range(6,-1,-1): g=jnp.where(sub==s,w[s],g)
        G[p]=jnp.where(lane<8*(p+1),g,0.0)
        return mine,w
    for t in range(n//2):
        p0,p1=2*t,2*t+1
        near=range(p1+1,min(p1+1+NEAR,n)); far=range(min(p1+1+NEAR,n),n)
        c0={q:[col_all(W[q],8*p0+k) for k in range(8)] for q in (p0,p1)}
        d1=[col_all(W[p1],8*p1+k) for k in range(8)]
        c0.update({q:[col_all(W[q],8*p0+k) for k in range(8)] for q in near})
        old=list(W)
        rs,l=small_chol([x+zero for x in c0[p0]])
        x=forward(c0[p1],rs,l)
        d1=[d1[k]-tree_sum([x[s]*row_all(x[s],k) for s in range(8)]) for k in range(8)]
        mine0,w=finish(p0,rs,l)
        W[p1]=jnp.where(mine0,0.0,W[p1])-tree_sum([x[s]*w[s] for s in range(8)])
        for q in near[:2]:
            y=forward(c0[q],rs,l)
            W[q]=jnp.where(mine0,0.0,W[q])-tree_sum([y[s]*w[s] for s in range(8)])
        v0=backward(w,rs,l)
        for q in near[2:]:
            W[q]=jnp.where(mine0,0.0,W[q])-tree_sum([c0[q][s]*v0[s] for s in range(8)])
        rs,l=small_chol(d1)
        c1={q:[col_all(W[q],8*p1+k) for k in range(8)] for q in near}
        mine1,w=finish(p1,rs,l)
        v1=backward(w,rs,l)
        for q in near:
            W[q]=jnp.where(mine1,0.0,W[q])-tree_sum([c1[q][s]*v1[s] for s in range(8)])
        if len(far):
            def pick(v):
                o=v[7]
                for s in range(6,-1,-1): o=jnp.where(sub==s,v[s],o)
                return o
            V0=pick(v0); V1=pick(v1)
            V0=jnp.where(mine1,0.0,V0)-tree_sum([col_all(V0,8*p1+k)*v1[k] for k in range(8)])
            z=jnp.zeros(REG,jnp.float32)
            rhs=jnp.concatenate([z]*p0+[V0,V1]+[z]*(n-p1-1),0)
            prod=lax.dot_general(jnp.concatenate([old[q] for q in far],0),rhs,(((1,),(0,)),((),())),precision=lax.Precision.HIGHEST,preferred_element_type=jnp.float32)
            for i,q in enumerate(far):
                W[q]=jnp.where(mine0|mine1,0.0,W[q])-prod[8*i:8*i+8]
    return G


def unpack_points(packed):
    n = packed.shape[0] // 16
    halves = packed.reshape(n, 16, 2 * F)
    return jnp.concatenate([halves[:, :, :F], halves[:, :, F:]], axis=1).reshape(32 * n, F)


def split(x):
    high = x.astype(jnp.bfloat16)
    rest = x - high.astype(jnp.float32)
    middle = rest.astype(jnp.bfloat16)
    low = (rest - middle.astype(jnp.float32)).astype(jnp.bfloat16)
    return high, middle, low


def stacked(a, b, dims=NN):
    n = a.shape[0]
    high, middle, low = split(a)
    b = split(b)
    first = dot16(jnp.concatenate([high, middle, low], axis=0), b[0], dims)
    second = dot16(jnp.concatenate([high, middle], axis=0), b[1], dims)
    small = first[2 * n :] + second[n:] + dot16(high, b[2], dims)
    return first[0:n] + (first[n : 2 * n] + second[0:n] + small)


def chained(a, b):
    a, b = split(a), split(b)
    left = jnp.concatenate([a[i] for i in (0, 0, 1, 1, 0, 2)], axis=1)
    right = jnp.concatenate([b[i] for i in (0, 1, 0, 1, 2, 0)], axis=0)
    return dot16(left, right, NN)


def spread_terms(parts, order, values, axis):
    shape = list(parts[0].shape)
    shape[axis] = TILE
    place = lax.broadcasted_iota(jnp.int32, shape, axis)
    tail = jnp.zeros(shape, jnp.float32)
    for i, v in enumerate(values):
        tail = jnp.where(place == i, v, tail)
    return jnp.concatenate([parts[i] for i in order] + [tail.astype(jnp.bfloat16)], axis=axis)


def as_float(parts):
    return [p.astype(jnp.float32) for p in parts]


LEFT = (0, 0, 1, 0, 1, 2)
RIGHT = (0, 1, 0, 2, 1, 0)


def left_terms(points, scales):
    weighted = points * scales
    sq = jnp.sum(weighted * points, axis=1, keepdims=True)
    return spread_terms(split(2.0 * weighted), LEFT, as_float(split(-sq)) + [1.0, 1.0, 1.0], 1)


def right_terms(points, sq, axis):
    return spread_terms(split(points), RIGHT, [1.0, 1.0, 1.0] + as_float(split(-sq)), axis)


def dot16(a, b, dims):
    return lax.dot_general(a, b, (dims, ((), ())), preferred_element_type=jnp.float32)


def panel_kernel(
    pan_ref, look_ref, scales_ref, rows_ref,
    diag_ref, panel_ref, update_ref,
    z_ref, left_ref, a_ref, g_ref, b_ref, right_ref, kern_ref, weight_ref,
):
    nb = B // TILE
    col, row = lax.axis_index("col"), lax.axis_index("row")
    scales = scales_ref[...]
    weight_ref[...] = jnp.broadcast_to(jnp.broadcast_to(scales, (8, F)).T[:, 0:1], (F, TILE))
    zero = jnp.full(REG, jnp.minimum(col, 0).astype(jnp.float32))
    points = unpack_points(pan_ref[...])
    look = unpack_points(look_ref[...])
    share = look.shape[0]
    left_ref[0:B] = left_terms(points, scales)
    left_ref[B : B + share] = left_terms(look, scales)
    others = jnp.concatenate([points, look, jnp.zeros((TILE - share, F), jnp.float32)], axis=0)
    right_ref[...] = right_terms(others, jnp.sum(others * others * scales, axis=1, keepdims=True), 1)
    for i in range(nb):
        at = slice(i * TILE, (i + 1) * TILE)
        block = jnp.exp(dot16(left_ref[at], right_ref[i * TILE :], NT))
        a_ref[at, i * TILE :] = block
        rid = lax.broadcasted_iota(jnp.int32, (TILE, TILE), 0)
        cid = lax.broadcasted_iota(jnp.int32, (TILE, TILE), 1)
        a_ref[at, at] = jnp.where(rid == cid, block[:, 0:TILE] + RIDGE, block[:, 0:TILE])
        if i % 2 == 1:
            a_ref[at, (i - 1) * TILE : i * TILE] = jnp.zeros((TILE, TILE), jnp.float32)

    wide = rows_ref.shape[1] // nb

    def after_tile(k):
        here = slice(k * TILE, (k + 1) * TILE)
        a_ref[here, k * TILE :] = chained(g_ref[k], a_ref[here, k * TILE :])
        if k % 2 == 0:
            later = slice((k + 1) * TILE, (k + 2) * TILE)
            a_ref[later, later.start :] -= mm(a_ref[here, later], a_ref[here, later.start :], TN)
        else:
            pair = slice((k - 1) * TILE, (k + 1) * TILE)
            for i in range(k + 1, nb, 2):
                later = slice(i * TILE, (i + 2) * TILE)
                a_ref[later, i * TILE :] -= mm(a_ref[pair, later], a_ref[pair, i * TILE :], TN)

    def step(k, carry):
        at = pl.multiple_of(k * TILE, TILE)
        G = factor_tile([a_ref[pl.ds(at + 8 * q, 8), pl.ds(at, TILE)] for q in range(TILE // 8)], zero)
        for q in range(TILE // 8):
            g_ref[k, 8 * q : 8 * q + 8, :] = G[q]
        to = pl.ds(pl.multiple_of(k * wide, wide), wide)
        rows = rows_ref[:, to]
        sq = jnp.sum(rows * rows * weight_ref[:, 0:1], axis=0, keepdims=True)
        kern_ref[:, to] = jnp.exp(dot16(left_ref[...], right_terms(rows, sq, 0), NN))
        lax.switch(k, [functools.partial(after_tile, i) for i in range(nb)])
        return carry

    lax.fori_loop(0, nb, step, 0)

    for k in range(nb):
        cols = slice(k * TILE, (k + 1) * TILE)
        r = lax.broadcasted_iota(jnp.int32, (share, TILE), 0) + col * share
        c = lax.broadcasted_iota(jnp.int32, (share, TILE), 1) + k * TILE
        b_ref[0:share, cols] = jnp.where(r == c, 1.0, 0.0).astype(jnp.float32)
        b_ref[share : 2 * share, cols] = a_ref[cols, B : B + TILE].T[0:share, :]
    for k in range(nb - 1, -1, -1):
        cols = slice(k * TILE, (k + 1) * TILE)
        z = stacked(b_ref[:, cols], g_ref[k])
        z_ref[:, cols] = z
        if k > 0:
            b_ref[:, 0 : k * TILE] = b_ref[:, 0 : k * TILE] - stacked(z, a_ref[0 : k * TILE, cols], NT)

    own = pl.ds(pl.multiple_of(col * share, share), share)
    to = pl.multiple_of(row * TILE, TILE)
    tile = a_ref[own, pl.ds(to, TILE)]
    r = lax.broadcasted_iota(jnp.int32, (share, TILE), 0) + col * share
    c = lax.broadcasted_iota(jnp.int32, (share, TILE), 1) + to
    diag_ref[...] = jnp.where(c >= r, tile, 0.0)

    block = 2 * wide

    def product(j, carry):
        to = pl.ds(pl.multiple_of(j * block, block), block)
        both = stacked(z_ref[...], kern_ref[0:B, to])
        panel_ref[:, to] = both[0:share]
        update_ref[:, to] = kern_ref[B : B + share, to] - both[share : 2 * share]
        return carry

    lax.fori_loop(0, rows_ref.shape[1] // block, product, 0)


def pack(points, copies):
    rows = jnp.broadcast_to(points.T, (copies,) + points.shape[::-1])
    return jnp.concatenate([rows[:, 0:16], rows[:, 16:32]], axis=2)


def local(panel, look, scales, row_points):
    share = 2 * look.shape[0]
    rows_dev = row_points.shape[1]
    vmem = pl.BlockSpec(memory_space=pltpu.VMEM)
    out = jax.ShapeDtypeStruct((share, rows_dev), jnp.float32)
    diag, panel_tile, updated = pl.pallas_call(
        panel_kernel,
        out_shape=(jax.ShapeDtypeStruct((share, B // 8), jnp.float32), out, out),
        in_specs=[vmem] * 4,
        out_specs=(vmem, vmem, vmem),
        scratch_shapes=[
            pltpu.VMEM((2 * share, B), jnp.float32),
            pltpu.VMEM((B + share, 4 * TILE), jnp.bfloat16),
            pltpu.VMEM((B, B + TILE), jnp.float32),
            pltpu.VMEM((B // TILE, TILE, TILE), jnp.float32),
            pltpu.VMEM((2 * share, B), jnp.float32),
            pltpu.VMEM((B + TILE, 4 * TILE), jnp.bfloat16),
            pltpu.VMEM((B + share, rows_dev), jnp.float32),
            pltpu.VMEM((F, TILE), jnp.float32),
        ],
        name="panel",
    )(panel, look, scales.reshape(1, F), row_points)
    return (diag.T, panel_tile, updated)


def body(row_points, panel_points, scales):
    n_col = lax.axis_size("col")
    n_row = lax.axis_size("row")
    col = lax.axis_index("col")
    row = lax.axis_index("row")
    share = B // n_col
    rows_dev = row_points.shape[1]
    first = col * share
    panel = lax.all_to_all(pack(panel_points, n_col), "col", 0, 0, tiled=True)
    panel = panel.reshape(B // 2, 2 * F)
    look = pack(lax.dynamic_slice_in_dim(row_points, first % rows_dev, share, 1), 1)[0]
    sent = [lax.ppermute(look, "row", [(0, to)]) for to in range(n_row - 2, 0, -2)]
    look = jnp.where(row == 0, look, sum(sent[1:], sent[0]))
    next_row = lax.ppermute(look, "row", [(i, i + 1) for i in range(0, n_row, 2)])
    look = jnp.where(row % 2 == 0, look, next_row)
    return local(panel, look, scales, row_points)


def solution(mesh):
    return jax.shard_map(
        body,
        mesh=mesh,
        in_specs=(P(None, "row"), P(None, "col"), P()),
        out_specs=(P("row", "col"), P("col", "row"), P("col", "row")),
        check_vma=False,
    )
```

```python
import functools

import jax
import jax.numpy as jnp
from jax import lax
from jax.experimental import pallas as pl
from jax.experimental.pallas import tpu as pltpu
from jax.sharding import PartitionSpec as P

B = 1024
F = 64
RIDGE = 0.5
TILE = 128
REG = (8, 128)
NEAR = 4
NN = ((1,), (0,))
TN = ((0,), (0,))
NT = ((1,), (1,))


def mm(a, b, dims):
    return lax.dot_general(
        a, b, (dims, ((), ())), precision=lax.Precision.HIGHEST, preferred_element_type=jnp.float32
    )


def row_all(x, i):
    return jnp.broadcast_to(x[i : i + 1, :], REG)


def col_all(x, j):
    return jnp.broadcast_to(x[:, j : j + 1], REG)


def tree_sum(xs):
    xs=list(xs)
    while len(xs)>1:
        xs=[xs[i]+xs[i+1] if i+1<len(xs) else xs[i] for i in range(0,len(xs),2)]
    return xs[0]

def small_chol(d):
    d=list(d)
    rs=[None]*8; l=[[None]*8 for _ in range(8)]
    for s in range(0,8,2):
        a,b,c=row_all(d[s],s),row_all(d[s],s+1),row_all(d[s+1],s+1)
        det=a*c-b*b
        r0=lax.rsqrt(a); rd=lax.rsqrt(det); inv=rd*rd
        rs[s]=r0; rs[s+1]=(a*r0)*rd
        y1=a*d[s+1]-b*d[s]
        l0=d[s]*r0; l1=y1*(r0*rd)
        for k in range(s+1,8): l[k][s]=row_all(l0,k)
        for k in range(s+2,8): l[k][s+1]=row_all(l1,k)
        if s<6:
            y0=c*d[s]-b*d[s+1]
            for m in range(s+2,8):
                d[m]=d[m]-(y0*row_all(d[s],m)+y1*row_all(d[s+1],m))*inv
    return rs,l
def forward(x,rs,l):
    x=list(x)
    for s in range(8):
        x[s]=x[s]*rs[s]
        for k in range(s+1,8): x[k]=x[k]-l[k][s]*x[s]
    return x
def backward(x,rs,l):
    x=list(x)
    for s in range(7,-1,-1):
        x[s]=x[s]*rs[s]
        for k in range(s): x[k]=x[k]-l[s][k]*x[s]
    return x

def factor_tile(W, zero):
    n=len(W); W=list(W)
    sub=lax.broadcasted_iota(jnp.int32,REG,0); lane=lax.broadcasted_iota(jnp.int32,REG,1)
    G=[None]*n
    def finish(p, rs, l):
        mine=lax.shift_right_logical(lane,3)==p
        w=jnp.where(mine, jnp.where(lane-8*p==sub,1.0,0.0).astype(jnp.float32), W[p])
        w=forward([row_all(w,s) for s in range(8)],rs,l)
        g=w[7]
        for s in range(6,-1,-1): g=jnp.where(sub==s,w[s],g)
        G[p]=jnp.where(lane<8*(p+1),g,0.0)
        return mine,w
    for t in range(n//2):
        p0,p1=2*t,2*t+1
        near=range(p1+1,min(p1+1+NEAR,n)); far=range(min(p1+1+NEAR,n),n)
        c0={q:[col_all(W[q],8*p0+k) for k in range(8)] for q in (p0,p1)}
        d1=[col_all(W[p1],8*p1+k) for k in range(8)]
        c0.update({q:[col_all(W[q],8*p0+k) for k in range(8)] for q in near})
        old=list(W)
        rs,l=small_chol([x+zero for x in c0[p0]])
        x=forward(c0[p1],rs,l)
        d1=[d1[k]-tree_sum([x[s]*row_all(x[s],k) for s in range(8)]) for k in range(8)]
        mine0,w=finish(p0,rs,l)
        W[p1]=jnp.where(mine0,0.0,W[p1])-tree_sum([x[s]*w[s] for s in range(8)])
        for q in near[:2]:
            y=forward(c0[q],rs,l)
            W[q]=jnp.where(mine0,0.0,W[q])-tree_sum([y[s]*w[s] for s in range(8)])
        v0=backward(w,rs,l)
        for q in near[2:]:
            W[q]=jnp.where(mine0,0.0,W[q])-tree_sum([c0[q][s]*v0[s] for s in range(8)])
        rs,l=small_chol(d1)
        c1={q:[col_all(W[q],8*p1+k) for k in range(8)] for q in near}
        mine1,w=finish(p1,rs,l)
        v1=backward(w,rs,l)
        for q in near:
            W[q]=jnp.where(mine1,0.0,W[q])-tree_sum([c1[q][s]*v1[s] for s in range(8)])
        if len(far):
            def pick(v):
                o=v[7]
                for s in range(6,-1,-1): o=jnp.where(sub==s,v[s],o)
                return o
            V0=pick(v0); V1=pick(v1)
            V0=jnp.where(mine1,0.0,V0)-tree_sum([col_all(V0,8*p1+k)*v1[k] for k in range(8)])
            z=jnp.zeros(REG,jnp.float32)
            rhs=jnp.concatenate([z]*p0+[V0,V1]+[z]*(n-p1-1),0)
            prod=lax.dot_general(jnp.concatenate([old[q] for q in far],0),rhs,(((1,),(0,)),((),())),precision=lax.Precision.HIGHEST,preferred_element_type=jnp.float32)
            for i,q in enumerate(far):
                W[q]=jnp.where(mine0|mine1,0.0,W[q])-prod[8*i:8*i+8]
    return G


def unpack_points(packed):
    n = packed.shape[0] // 16
    halves = packed.reshape(n, 16, 2 * F)
    return jnp.concatenate([halves[:, :, :F], halves[:, :, F:]], axis=1).reshape(32 * n, F)


def split(x):
    high = x.astype(jnp.bfloat16)
    rest = x - high.astype(jnp.float32)
    middle = rest.astype(jnp.bfloat16)
    low = (rest - middle.astype(jnp.float32)).astype(jnp.bfloat16)
    return high, middle, low


def stacked(a, b, dims=NN):
    n = a.shape[0]
    high, middle, low = split(a)
    b = split(b)
    first = dot16(jnp.concatenate([high, middle, low], axis=0), b[0], dims)
    second = dot16(jnp.concatenate([high, middle], axis=0), b[1], dims)
    small = first[2 * n :] + second[n:] + dot16(high, b[2], dims)
    return first[0:n] + (first[n : 2 * n] + second[0:n] + small)


def chained(a, b):
    a, b = split(a), split(b)
    left = jnp.concatenate([a[i] for i in (0, 0, 1, 1, 0, 2)], axis=1)
    right = jnp.concatenate([b[i] for i in (0, 1, 0, 1, 2, 0)], axis=0)
    return dot16(left, right, NN)


def spread_terms(parts, order, values, first_one, axis):
    shape = list(parts[0].shape)
    shape[axis] = TILE
    place = lax.broadcasted_iota(jnp.int32, shape, axis)
    tail = jnp.where((place >= first_one) & (place < first_one + 3), 1.0, 0.0).astype(jnp.float32)
    for i, v in enumerate(values):
        tail = jnp.where(place == 3 - first_one + i, v, tail)
    return jnp.concatenate([parts[i] for i in order] + [tail.astype(jnp.bfloat16)], axis=axis)


def as_float(parts):
    return [p.astype(jnp.float32) for p in parts]


LEFT = (0, 0, 1, 0, 1, 2)
RIGHT = (0, 1, 0, 2, 1, 0)


def left_terms(points, scales):
    weighted = points * scales
    sq = jnp.sum(weighted * points, axis=1, keepdims=True)
    return spread_terms(split(2.0 * weighted), LEFT, as_float(split(-sq)), 3, 1)


def right_terms(points, sq, axis):
    return spread_terms(split(points), RIGHT, as_float(split(-sq)), 0, axis)


def dot16(a, b, dims):
    return lax.dot_general(a, b, (dims, ((), ())), preferred_element_type=jnp.float32)


def panel_kernel(
    pan_ref, look_ref, scales_ref, rows_ref,
    diag_ref, panel_ref, update_ref,
    z_ref, left_ref, a_ref, g_ref, b_ref, right_ref, kern_ref, weight_ref,
):
    nb = B // TILE
    col, row = lax.axis_index("col"), lax.axis_index("row")
    scales = scales_ref[...]
    weight_ref[...] = jnp.broadcast_to(jnp.broadcast_to(scales, (8, F)).T[:, 0:1], (F, TILE))
    zero = jnp.full(REG, jnp.minimum(col, 0).astype(jnp.float32))
    points = unpack_points(pan_ref[...])
    look = unpack_points(look_ref[...])
    share = look.shape[0]
    left_ref[0:B] = left_terms(points, scales)
    left_ref[B : B + share] = left_terms(look, scales)
    others = jnp.concatenate([points, look, jnp.zeros((TILE - share, F), jnp.float32)], axis=0)
    right_ref[...] = right_terms(others, jnp.sum(others * others * scales, axis=1, keepdims=True), 1)
    for i in range(nb):
        at = slice(i * TILE, (i + 1) * TILE)
        block = jnp.exp(dot16(left_ref[at], right_ref[i * TILE :], NT))
        a_ref[at, i * TILE :] = block
        rid = lax.broadcasted_iota(jnp.int32, (TILE, TILE), 0)
        cid = lax.broadcasted_iota(jnp.int32, (TILE, TILE), 1)
        a_ref[at, at] = jnp.where(rid == cid, block[:, 0:TILE] + RIDGE, block[:, 0:TILE])
        if i % 2 == 1:
            a_ref[at, (i - 1) * TILE : i * TILE] = jnp.zeros((TILE, TILE), jnp.float32)

    wide = rows_ref.shape[1] // nb

    def after_tile(k):
        here = slice(k * TILE, (k + 1) * TILE)
        a_ref[here, k * TILE :] = chained(g_ref[k], a_ref[here, k * TILE :])
        if k % 2 == 0:
            later = slice((k + 1) * TILE, (k + 2) * TILE)
            a_ref[later, later.start :] -= mm(a_ref[here, later], a_ref[here, later.start :], TN)
        else:
            pair = slice((k - 1) * TILE, (k + 1) * TILE)
            for i in range(k + 1, nb, 2):
                later = slice(i * TILE, (i + 2) * TILE)
                a_ref[later, i * TILE :] -= mm(a_ref[pair, later], a_ref[pair, i * TILE :], TN)

    def step(k, carry):
        at = pl.multiple_of(k * TILE, TILE)
        G = factor_tile([a_ref[pl.ds(at + 8 * q, 8), pl.ds(at, TILE)] for q in range(TILE // 8)], zero)
        for q in range(TILE // 8):
            g_ref[k, 8 * q : 8 * q + 8, :] = G[q]
        to = pl.ds(pl.multiple_of(k * wide, wide), wide)
        rows = rows_ref[:, to]
        sq = jnp.sum(rows * rows * weight_ref[:, 0:1], axis=0, keepdims=True)
        kern_ref[:, to] = jnp.exp(dot16(left_ref[...], right_terms(rows, sq, 0), NN))
        lax.switch(k, [functools.partial(after_tile, i) for i in range(nb)])
        return carry

    lax.fori_loop(0, nb, step, 0)

    for k in range(nb):
        cols = slice(k * TILE, (k + 1) * TILE)
        r = lax.broadcasted_iota(jnp.int32, (share, TILE), 0) + col * share
        c = lax.broadcasted_iota(jnp.int32, (share, TILE), 1) + k * TILE
        b_ref[0:share, cols] = jnp.where(r == c, 1.0, 0.0).astype(jnp.float32)
        b_ref[share : 2 * share, cols] = a_ref[cols, B : B + TILE].T[0:share, :]
    for k in range(nb - 1, -1, -1):
        cols = slice(k * TILE, (k + 1) * TILE)
        z = stacked(b_ref[:, cols], g_ref[k])
        z_ref[:, cols] = z
        if k > 0:
            b_ref[:, 0 : k * TILE] = b_ref[:, 0 : k * TILE] - stacked(z, a_ref[0 : k * TILE, cols], NT)

    own = pl.ds(pl.multiple_of(col * share, share), share)
    to = pl.multiple_of(row * TILE, TILE)
    tile = a_ref[own, pl.ds(to, TILE)]
    r = lax.broadcasted_iota(jnp.int32, (share, TILE), 0) + col * share
    c = lax.broadcasted_iota(jnp.int32, (share, TILE), 1) + to
    diag_ref[...] = jnp.where(c >= r, tile, 0.0)

    block = 2 * wide

    def product(j, carry):
        to = pl.ds(pl.multiple_of(j * block, block), block)
        both = stacked(z_ref[...], kern_ref[0:B, to])
        panel_ref[:, to] = both[0:share]
        update_ref[:, to] = kern_ref[B : B + share, to] - both[share : 2 * share]
        return carry

    lax.fori_loop(0, rows_ref.shape[1] // block, product, 0)


def pack(points, copies):
    rows = jnp.broadcast_to(points.T, (copies,) + points.shape[::-1])
    first = lax.pad(rows, 0.0, ((0, 0, 0), (0, -16, 0), (0, F, 0)))
    second = lax.pad(rows, 0.0, ((0, 0, 0), (-16, 0, 0), (F, 0, 0)))
    return first + second


def local(panel, look, scales, row_points):
    share = 2 * look.shape[0]
    rows_dev = row_points.shape[1]
    vmem = pl.BlockSpec(memory_space=pltpu.VMEM)
    out = jax.ShapeDtypeStruct((share, rows_dev), jnp.float32)
    diag, panel_tile, updated = pl.pallas_call(
        panel_kernel,
        out_shape=(jax.ShapeDtypeStruct((share, B // 8), jnp.float32), out, out),
        in_specs=[vmem] * 4,
        out_specs=(vmem, vmem, vmem),
        scratch_shapes=[
            pltpu.VMEM((2 * share, B), jnp.float32),
            pltpu.VMEM((B + share, 4 * TILE), jnp.bfloat16),
            pltpu.VMEM((B, B + TILE), jnp.float32),
            pltpu.VMEM((B // TILE, TILE, TILE), jnp.float32),
            pltpu.VMEM((2 * share, B), jnp.float32),
            pltpu.VMEM((B + TILE, 4 * TILE), jnp.bfloat16),
            pltpu.VMEM((B + share, rows_dev), jnp.float32),
            pltpu.VMEM((F, TILE), jnp.float32),
        ],
        name="panel",
    )(panel, look, scales.reshape(1, F), row_points)
    return (diag.T, panel_tile, updated)


def body(row_points, panel_points, scales):
    n_col = lax.axis_size("col")
    n_row = lax.axis_size("row")
    col = lax.axis_index("col")
    row = lax.axis_index("row")
    share = B // n_col
    rows_dev = row_points.shape[1]
    first = col * share
    panel = lax.all_to_all(pack(panel_points, n_col), "col", 0, 0, tiled=True)
    panel = panel.reshape(B // 2, 2 * F)
    look = pack(lax.dynamic_slice_in_dim(row_points, first % rows_dev, share, 1), 1)[0]
    sent = [lax.ppermute(look, "row", [(0, to)]) for to in range(n_row - 2, 0, -2)]
    look = jnp.where(row == 0, look, sum(sent[1:], sent[0]))
    next_row = lax.ppermute(look, "row", [(i, i + 1) for i in range(0, n_row, 2)])
    look = jnp.where(row % 2 == 0, look, next_row)
    return local(panel, look, scales, row_points)


def solution(mesh):
    return jax.shard_map(
        body,
        mesh=mesh,
        in_specs=(P(None, "row"), P(None, "col"), P()),
        out_specs=(P("row", "col"), P("col", "row"), P("col", "row")),
        check_vma=False,
    )
```

```python
import functools

import jax
import jax.numpy as jnp
from jax import lax
from jax.experimental import pallas as pl
from jax.experimental.pallas import tpu as pltpu
from jax.sharding import PartitionSpec as P

B = 1024
F = 64
RIDGE = 0.5
TILE = 128
REG = (8, 128)
NEAR = 4
NN = ((1,), (0,))
TN = ((0,), (0,))
NT = ((1,), (1,))


def mm(a, b, dims):
    return lax.dot_general(
        a, b, (dims, ((), ())), precision=lax.Precision.HIGHEST, preferred_element_type=jnp.float32
    )


def row_all(x, i):
    return jnp.broadcast_to(x[i : i + 1, :], REG)


def col_all(x, j):
    return jnp.broadcast_to(x[:, j : j + 1], REG)


def tree_sum(xs):
    xs=list(xs)
    while len(xs)>1:
        xs=[xs[i]+xs[i+1] if i+1<len(xs) else xs[i] for i in range(0,len(xs),2)]
    return xs[0]

def small_chol(d):
    d=list(d)
    rs=[None]*8; l=[[None]*8 for _ in range(8)]
    for s in range(0,8,2):
        a,b,c=row_all(d[s],s),row_all(d[s],s+1),row_all(d[s+1],s+1)
        det=a*c-b*b
        r0=lax.rsqrt(a); rd=lax.rsqrt(det); inv=rd*rd
        rs[s]=r0; rs[s+1]=(a*r0)*rd
        y1=a*d[s+1]-b*d[s]
        l0=d[s]*r0; l1=y1*(r0*rd)
        for k in range(s+1,8): l[k][s]=row_all(l0,k)
        for k in range(s+2,8): l[k][s+1]=row_all(l1,k)
        if s<6:
            y0=c*d[s]-b*d[s+1]
            for m in range(s+2,8):
                d[m]=d[m]-(y0*row_all(d[s],m)+y1*row_all(d[s+1],m))*inv
    return rs,l
def forward(x,rs,l):
    x=list(x)
    for s in range(8):
        x[s]=x[s]*rs[s]
        for k in range(s+1,8): x[k]=x[k]-l[k][s]*x[s]
    return x
def backward(x,rs,l):
    x=list(x)
    for s in range(7,-1,-1):
        x[s]=x[s]*rs[s]
        for k in range(s): x[k]=x[k]-l[s][k]*x[s]
    return x

def factor_tile(W, zero):
    n=len(W); W=list(W)
    sub=lax.broadcasted_iota(jnp.int32,REG,0); lane=lax.broadcasted_iota(jnp.int32,REG,1)
    G=[None]*n
    def finish(p, rs, l):
        mine=lax.shift_right_logical(lane,3)==p
        w=jnp.where(mine, jnp.where(lane-8*p==sub,1.0,0.0).astype(jnp.float32), W[p])
        w=forward([row_all(w,s) for s in range(8)],rs,l)
        g=w[7]
        for s in range(6,-1,-1): g=jnp.where(sub==s,w[s],g)
        G[p]=jnp.where(lane<8*(p+1),g,0.0)
        return mine,w
    for t in range(n//2):
        p0,p1=2*t,2*t+1
        near=range(p1+1,min(p1+1+NEAR,n)); far=range(min(p1+1+NEAR,n),n)
        c0={p0:[],p1:[]}
        for k in range(8):
            c0[p0].append(col_all(W[p0],8*p0+k)); c0[p1].append(col_all(W[p1],8*p0+k))
        d1=[col_all(W[p1],8*p1+k) for k in range(8)]
        c0.update({q:[col_all(W[q],8*p0+k) for k in range(8)] for q in near})
        old=list(W)
        rs,l=small_chol([x+zero for x in c0[p0]])
        x=forward(c0[p1],rs,l)
        d1=[d1[k]-tree_sum([x[s]*row_all(x[s],k) for s in range(8)]) for k in range(8)]
        mine0,w=finish(p0,rs,l)
        W[p1]=jnp.where(mine0,0.0,W[p1])-tree_sum([x[s]*w[s] for s in range(8)])
        v0=backward(w,rs,l)
        for q in near:
            W[q]=jnp.where(mine0,0.0,W[q])-tree_sum([c0[q][s]*v0[s] for s in range(8)])
        rs,l=small_chol(d1)
        c1={q:[col_all(W[q],8*p1+k) for k in range(8)] for q in near}
        mine1,w=finish(p1,rs,l)
        v1=backward(w,rs,l)
        for q in near:
            W[q]=jnp.where(mine1,0.0,W[q])-tree_sum([c1[q][s]*v1[s] for s in range(8)])
        if len(far):
            def pick(v):
                o=v[7]
                for s in range(6,-1,-1): o=jnp.where(sub==s,v[s],o)
                return o
            V0=pick(v0); V1=pick(v1)
            V0=jnp.where(mine1,0.0,V0)-tree_sum([col_all(V0,8*p1+k)*v1[k] for k in range(8)])
            z=jnp.zeros(REG,jnp.float32)
            rhs=jnp.concatenate([z]*p0+[V0,V1]+[z]*(n-p1-1),0)
            prod=lax.dot_general(jnp.concatenate([old[q] for q in far],0),rhs,(((1,),(0,)),((),())),precision=lax.Precision.HIGHEST,preferred_element_type=jnp.float32)
            for i,q in enumerate(far):
                W[q]=jnp.where(mine0|mine1,0.0,W[q])-prod[8*i:8*i+8]
    return G


def unpack_points(packed):
    n = packed.shape[0] // 16
    halves = packed.reshape(n, 16, 2 * F)
    return jnp.concatenate([halves[:, :, :F], halves[:, :, F:]], axis=1).reshape(32 * n, F)


def split(x):
    high = x.astype(jnp.bfloat16)
    rest = x - high.astype(jnp.float32)
    middle = rest.astype(jnp.bfloat16)
    low = (rest - middle.astype(jnp.float32)).astype(jnp.bfloat16)
    return high, middle, low


def stacked(a, b, dims=NN):
    n = a.shape[0]
    high, middle, low = split(a)
    b = split(b)
    first = dot16(jnp.concatenate([high, middle, low], axis=0), b[0], dims)
    second = dot16(jnp.concatenate([high, middle], axis=0), b[1], dims)
    small = first[2 * n :] + second[n:] + dot16(high, b[2], dims)
    return first[0:n] + (first[n : 2 * n] + second[0:n] + small)


def chained(a, b):
    a, b = split(a), split(b)
    left = jnp.concatenate([a[i] for i in (0, 0, 1, 1, 0, 2)], axis=1)
    right = jnp.concatenate([b[i] for i in (0, 1, 0, 1, 2, 0)], axis=0)
    return dot16(left, right, NN)


def spread_terms(parts, order, values, axis):
    shape = list(parts[0].shape)
    shape[axis] = TILE
    place = lax.broadcasted_iota(jnp.int32, shape, axis)
    tail = jnp.zeros(shape, jnp.float32)
    for i, v in enumerate(values):
        tail = jnp.where(place == i, v, tail)
    return jnp.concatenate([parts[i] for i in order] + [tail.astype(jnp.bfloat16)], axis=axis)


def as_float(parts):
    return [p.astype(jnp.float32) for p in parts]


LEFT = (0, 0, 1, 0, 1, 2)
RIGHT = (0, 1, 0, 2, 1, 0)


def left_terms(points, scales):
    weighted = points * scales
    sq = jnp.sum(weighted * points, axis=1, keepdims=True)
    return spread_terms(split(2.0 * weighted), LEFT, as_float(split(-sq)) + [1.0, 1.0, 1.0], 1)


def right_terms(points, sq, axis):
    return spread_terms(split(points), RIGHT, [1.0, 1.0, 1.0] + as_float(split(-sq)), axis)


def dot16(a, b, dims):
    return lax.dot_general(a, b, (dims, ((), ())), preferred_element_type=jnp.float32)


def panel_kernel(
    pan_ref, look_ref, scales_ref, rows_ref,
    diag_ref, panel_ref, update_ref,
    z_ref, left_ref, a_ref, g_ref, b_ref, right_ref, kern_ref, weight_ref,
):
    nb = B // TILE
    col, row = lax.axis_index("col"), lax.axis_index("row")
    scales = scales_ref[...]
    weight_ref[...] = jnp.broadcast_to(jnp.broadcast_to(scales, (8, F)).T[:, 0:1], (F, TILE))
    zero = jnp.full(REG, jnp.minimum(col, 0).astype(jnp.float32))
    points = unpack_points(pan_ref[...])
    look = unpack_points(look_ref[...])
    share = look.shape[0]
    left_ref[0:B] = left_terms(points, scales)
    left_ref[B : B + share] = left_terms(look, scales)
    others = jnp.concatenate([points, look, jnp.zeros((TILE - share, F), jnp.float32)], axis=0)
    right_ref[...] = right_terms(others, jnp.sum(others * others * scales, axis=1, keepdims=True), 1)
    for i in range(nb):
        at = slice(i * TILE, (i + 1) * TILE)
        block = jnp.exp(dot16(left_ref[at], right_ref[i * TILE :], NT))
        a_ref[at, i * TILE :] = block
        rid = lax.broadcasted_iota(jnp.int32, (TILE, TILE), 0)
        cid = lax.broadcasted_iota(jnp.int32, (TILE, TILE), 1)
        a_ref[at, at] = jnp.where(rid == cid, block[:, 0:TILE] + RIDGE, block[:, 0:TILE])
        if i % 2 == 1:
            a_ref[at, (i - 1) * TILE : i * TILE] = jnp.zeros((TILE, TILE), jnp.float32)

    wide = rows_ref.shape[1] // nb

    def after_tile(k):
        here = slice(k * TILE, (k + 1) * TILE)
        a_ref[here, k * TILE :] = chained(g_ref[k], a_ref[here, k * TILE :])
        if k % 2 == 0:
            later = slice((k + 1) * TILE, (k + 2) * TILE)
            a_ref[later, later.start :] -= mm(a_ref[here, later], a_ref[here, later.start :], TN)
        else:
            pair = slice((k - 1) * TILE, (k + 1) * TILE)
            for i in range(k + 1, nb, 2):
                later = slice(i * TILE, (i + 2) * TILE)
                a_ref[later, i * TILE :] -= mm(a_ref[pair, later], a_ref[pair, i * TILE :], TN)

    def step(k, carry):
        at = pl.multiple_of(k * TILE, TILE)
        G = factor_tile([a_ref[pl.ds(at + 8 * q, 8), pl.ds(at, TILE)] for q in range(TILE // 8)], zero)
        for q in range(TILE // 8):
            g_ref[k, 8 * q : 8 * q + 8, :] = G[q]
        to = pl.ds(pl.multiple_of(k * wide, wide), wide)
        rows = rows_ref[:, to]
        sq = jnp.sum(rows * rows * weight_ref[:, 0:1], axis=0, keepdims=True)
        kern_ref[:, to] = jnp.exp(dot16(left_ref[...], right_terms(rows, sq, 0), NN))
        lax.switch(k, [functools.partial(after_tile, i) for i in range(nb)])
        return carry

    lax.fori_loop(0, nb, step, 0)

    for k in range(nb):
        cols = slice(k * TILE, (k + 1) * TILE)
        r = lax.broadcasted_iota(jnp.int32, (share, TILE), 0) + col * share
        c = lax.broadcasted_iota(jnp.int32, (share, TILE), 1) + k * TILE
        b_ref[0:share, cols] = jnp.where(r == c, 1.0, 0.0).astype(jnp.float32)
        b_ref[share : 2 * share, cols] = a_ref[cols, B : B + TILE].T[0:share, :]
    for k in range(nb - 1, -1, -1):
        cols = slice(k * TILE, (k + 1) * TILE)
        z = stacked(b_ref[:, cols], g_ref[k])
        z_ref[:, cols] = z
        if k > 0:
            b_ref[:, 0 : k * TILE] = b_ref[:, 0 : k * TILE] - stacked(z, a_ref[0 : k * TILE, cols], NT)

    own = pl.ds(pl.multiple_of(col * share, share), share)
    to = pl.multiple_of(row * TILE, TILE)
    tile = a_ref[own, pl.ds(to, TILE)]
    r = lax.broadcasted_iota(jnp.int32, (share, TILE), 0) + col * share
    c = lax.broadcasted_iota(jnp.int32, (share, TILE), 1) + to
    diag_ref[...] = jnp.where(c >= r, tile, 0.0)

    block = 2 * wide

    def product(j, carry):
        to = pl.ds(pl.multiple_of(j * block, block), block)
        both = stacked(z_ref[...], kern_ref[0:B, to])
        panel_ref[:, to] = both[0:share]
        update_ref[:, to] = kern_ref[B : B + share, to] - both[share : 2 * share]
        return carry

    lax.fori_loop(0, rows_ref.shape[1] // block, product, 0)


def pack(points, copies):
    rows = jnp.broadcast_to(points.T, (copies,) + points.shape[::-1])
    return jnp.concatenate([rows[:, 0:16], rows[:, 16:32]], axis=2)


def local(panel, look, scales, row_points):
    share = 2 * look.shape[0]
    rows_dev = row_points.shape[1]
    vmem = pl.BlockSpec(memory_space=pltpu.VMEM)
    out = jax.ShapeDtypeStruct((share, rows_dev), jnp.float32)
    diag, panel_tile, updated = pl.pallas_call(
        panel_kernel,
        out_shape=(jax.ShapeDtypeStruct((share, B // 8), jnp.float32), out, out),
        in_specs=[vmem] * 4,
        out_specs=(vmem, vmem, vmem),
        scratch_shapes=[
            pltpu.VMEM((2 * share, B), jnp.float32),
            pltpu.VMEM((B + share, 4 * TILE), jnp.bfloat16),
            pltpu.VMEM((B, B + TILE), jnp.float32),
            pltpu.VMEM((B // TILE, TILE, TILE), jnp.float32),
            pltpu.VMEM((2 * share, B), jnp.float32),
            pltpu.VMEM((B + TILE, 4 * TILE), jnp.bfloat16),
            pltpu.VMEM((B + share, rows_dev), jnp.float32),
            pltpu.VMEM((F, TILE), jnp.float32),
        ],
        name="panel",
    )(panel, look, scales.reshape(1, F), row_points)
    return (diag.T, panel_tile, updated)


def body(row_points, panel_points, scales):
    n_col = lax.axis_size("col")
    n_row = lax.axis_size("row")
    col = lax.axis_index("col")
    row = lax.axis_index("row")
    share = B // n_col
    rows_dev = row_points.shape[1]
    first = col * share
    panel = lax.all_to_all(pack(panel_points, n_col), "col", 0, 0, tiled=True)
    panel = panel.reshape(B // 2, 2 * F)
    look = pack(lax.dynamic_slice_in_dim(row_points, first % rows_dev, share, 1), 1)[0]
    sent = [lax.ppermute(look, "row", [(0, to)]) for to in range(n_row - 2, 0, -2)]
    look = jnp.where(row == 0, look, sum(sent[1:], sent[0]))
    next_row = lax.ppermute(look, "row", [(i, i + 1) for i in range(0, n_row, 2)])
    look = jnp.where(row % 2 == 0, look, next_row)
    return local(panel, look, scales, row_points)


def solution(mesh):
    return jax.shard_map(
        body,
        mesh=mesh,
        in_specs=(P(None, "row"), P(None, "col"), P()),
        out_specs=(P("row", "col"), P("col", "row"), P("col", "row")),
        check_vma=False,
    )
```

```python
import functools

import jax
import jax.numpy as jnp
from jax import lax
from jax.experimental import pallas as pl
from jax.experimental.pallas import tpu as pltpu
from jax.sharding import PartitionSpec as P

B = 1024
F = 64
RIDGE = 0.5
TILE = 128
REG = (8, 128)
NEAR = 4
NN = ((1,), (0,))
TN = ((0,), (0,))
NT = ((1,), (1,))


def mm(a, b, dims):
    return lax.dot_general(
        a, b, (dims, ((), ())), precision=lax.Precision.HIGHEST, preferred_element_type=jnp.float32
    )


def row_all(x, i):
    return jnp.broadcast_to(x[i : i + 1, :], REG)


def col_all(x, j):
    return jnp.broadcast_to(x[:, j : j + 1], REG)


def tree_sum(xs):
    xs=list(xs)
    while len(xs)>1:
        xs=[xs[i]+xs[i+1] if i+1<len(xs) else xs[i] for i in range(0,len(xs),2)]
    return xs[0]

def small_chol(d):
    d=list(d)
    rs=[None]*8; l=[[None]*8 for _ in range(8)]
    for s in range(0,8,2):
        a,b,c=row_all(d[s],s),row_all(d[s],s+1),row_all(d[s+1],s+1)
        det=a*c-b*b
        r0=lax.rsqrt(a); rd=lax.rsqrt(det); inv=rd*rd
        rs[s]=r0; rs[s+1]=(a*r0)*rd
        y1=a*d[s+1]-b*d[s]
        l0=d[s]*r0; l1=y1*(r0*rd)
        for k in range(s+1,8): l[k][s]=row_all(l0,k)
        for k in range(s+2,8): l[k][s+1]=row_all(l1,k)
        if s<6:
            y0=c*d[s]-b*d[s+1]
            for m in range(s+2,8):
                d[m]=d[m]-(y0*row_all(d[s],m)+y1*row_all(d[s+1],m))*inv
    return rs,l
def forward(x,rs,l):
    x=list(x)
    for s in range(8):
        x[s]=x[s]*rs[s]
        for k in range(s+1,8): x[k]=x[k]-l[k][s]*x[s]
    return x
def backward(x,rs,l):
    x=list(x)
    for s in range(7,-1,-1):
        x[s]=x[s]*rs[s]
        for k in range(s): x[k]=x[k]-l[s][k]*x[s]
    return x

def factor_tile(W, zero):
    n=len(W); W=list(W)
    sub=lax.broadcasted_iota(jnp.int32,REG,0); lane=lax.broadcasted_iota(jnp.int32,REG,1)
    G=[None]*n
    def finish(p, rs, l):
        mine=lax.shift_right_logical(lane,3)==p
        w=jnp.where(mine, jnp.where(lane-8*p==sub,1.0,0.0).astype(jnp.float32), W[p])
        w=forward([row_all(w,s) for s in range(8)],rs,l)
        g=w[7]
        for s in range(6,-1,-1): g=jnp.where(sub==s,w[s],g)
        G[p]=jnp.where(lane<8*(p+1),g,0.0)
        return mine,w
    for t in range(n//2):
        p0,p1=2*t,2*t+1
        near=range(p1+1,min(p1+1+NEAR,n)); far=range(min(p1+1+NEAR,n),n)
        c0={p0:[],p1:[]}
        for k in range(8):
            c0[p0].append(col_all(W[p0],8*p0+k)); c0[p1].append(col_all(W[p1],8*p0+k))
        d1=[col_all(W[p1],8*p1+k) for k in range(8)]
        c0.update({q:[col_all(W[q],8*p0+k) for k in range(8)] for q in near})
        old=list(W)
        rs,l=small_chol([x+zero for x in c0[p0]])
        x=forward(c0[p1],rs,l)
        d1=[d1[k]-tree_sum([x[s]*row_all(x[s],k) for s in range(8)]) for k in range(8)]
        mine0,w=finish(p0,rs,l)
        W[p1]=jnp.where(mine0,0.0,W[p1])-tree_sum([x[s]*w[s] for s in range(8)])
        v0=backward(w,rs,l)
        for q in near:
            W[q]=jnp.where(mine0,0.0,W[q])-tree_sum([c0[q][s]*v0[s] for s in range(8)])
        rs,l=small_chol(d1)
        c1={q:[col_all(W[q],8*p1+k) for k in range(8)] for q in near}
        mine1,w=finish(p1,rs,l)
        v1=backward(w,rs,l)
        for q in near:
            W[q]=jnp.where(mine1,0.0,W[q])-tree_sum([c1[q][s]*v1[s] for s in range(8)])
        if len(far):
            def pick(v):
                o=v[7]
                for s in range(6,-1,-1): o=jnp.where(sub==s,v[s],o)
                return o
            V0=pick(v0); V1=pick(v1)
            V0=jnp.where(mine1,0.0,V0)-tree_sum([col_all(V0,8*p1+k)*v1[k] for k in range(8)])
            z=jnp.zeros(REG,jnp.float32)
            rhs=jnp.concatenate([z]*p0+[V0,V1]+[z]*(n-p1-1),0)
            prod=lax.dot_general(jnp.concatenate([old[q] for q in far],0),rhs,(((1,),(0,)),((),())),precision=lax.Precision.HIGHEST,preferred_element_type=jnp.float32)
            for i,q in enumerate(far):
                W[q]=jnp.where(mine0|mine1,0.0,W[q])-prod[8*i:8*i+8]
    return G


def unpack_points(packed):
    n = packed.shape[0] // 16
    halves = packed.reshape(n, 16, 2 * F)
    return jnp.concatenate([halves[:, :, :F], halves[:, :, F:]], axis=1).reshape(32 * n, F)


def split(x):
    high = x.astype(jnp.bfloat16)
    rest = x - high.astype(jnp.float32)
    middle = rest.astype(jnp.bfloat16)
    low = (rest - middle.astype(jnp.float32)).astype(jnp.bfloat16)
    return high, middle, low


def stacked(a, b, dims=NN):
    n = a.shape[0]
    high, middle, low = split(a)
    b = split(b)
    first = dot16(jnp.concatenate([high, middle, low], axis=0), b[0], dims)
    second = dot16(jnp.concatenate([high, middle], axis=0), b[1], dims)
    small = first[2 * n :] + second[n:] + dot16(high, b[2], dims)
    return first[0:n] + (first[n : 2 * n] + second[0:n] + small)


def chained(a, b):
    a, b = split(a), split(b)
    left = jnp.concatenate([a[i] for i in (0, 0, 1, 1, 0, 2)], axis=1)
    right = jnp.concatenate([b[i] for i in (0, 1, 0, 1, 2, 0)], axis=0)
    return dot16(left, right, NN)


def spread_terms(parts, order, values, axis):
    shape = list(parts[0].shape)
    shape[axis] = TILE
    place = lax.broadcasted_iota(jnp.int32, shape, axis)
    tail = jnp.zeros(shape, jnp.float32)
    for i, v in enumerate(values):
        tail = jnp.where(place == i, v, tail)
    return jnp.concatenate([parts[i] for i in order] + [tail.astype(jnp.bfloat16)], axis=axis)


def as_float(parts):
    return [p.astype(jnp.float32) for p in parts]


LEFT = (0, 0, 1, 0, 1, 2)
RIGHT = (0, 1, 0, 2, 1, 0)


def left_terms(points, scales):
    weighted = points * scales
    sq = jnp.sum(weighted * points, axis=1, keepdims=True)
    return spread_terms(split(2.0 * weighted), LEFT, as_float(split(-sq)) + [1.0, 1.0, 1.0], 1)


def right_terms(points, sq, axis):
    return spread_terms(split(points), RIGHT, [1.0, 1.0, 1.0] + as_float(split(-sq)), axis)


def dot16(a, b, dims):
    return lax.dot_general(a, b, (dims, ((), ())), preferred_element_type=jnp.float32)


def panel_kernel(
    pan_ref, look_ref, sent_ref, scales_ref, rows_ref,
    diag_ref, panel_ref, update_ref,
    z_ref, left_ref, a_ref, g_ref, b_ref, right_ref, kern_ref, weight_ref,
):
    nb = B // TILE
    col, row = lax.axis_index("col"), lax.axis_index("row")
    scales = scales_ref[...]
    weight_ref[...] = jnp.broadcast_to(jnp.broadcast_to(scales, (8, F)).T[:, 0:1], (F, TILE))
    zero = jnp.full(REG, jnp.minimum(col, 0).astype(jnp.float32))
    points = unpack_points(pan_ref[...])
    look = unpack_points(jnp.where(row % 2 == 0, look_ref[...], sent_ref[...]))
    share = look.shape[0]
    left_ref[0:B] = left_terms(points, scales)
    left_ref[B : B + share] = left_terms(look, scales)
    others = jnp.concatenate([points, look, jnp.zeros((TILE - share, F), jnp.float32)], axis=0)
    right_ref[...] = right_terms(others, jnp.sum(others * others * scales, axis=1, keepdims=True), 1)
    for i in range(nb):
        at = slice(i * TILE, (i + 1) * TILE)
        block = jnp.exp(dot16(left_ref[at], right_ref[i * TILE :], NT))
        a_ref[at, i * TILE :] = block
        rid = lax.broadcasted_iota(jnp.int32, (TILE, TILE), 0)
        cid = lax.broadcasted_iota(jnp.int32, (TILE, TILE), 1)
        a_ref[at, at] = jnp.where(rid == cid, block[:, 0:TILE] + RIDGE, block[:, 0:TILE])
        if i % 2 == 1:
            a_ref[at, (i - 1) * TILE : i * TILE] = jnp.zeros((TILE, TILE), jnp.float32)

    wide = rows_ref.shape[1] // nb

    def after_tile(k):
        here = slice(k * TILE, (k + 1) * TILE)
        a_ref[here, k * TILE :] = chained(g_ref[k], a_ref[here, k * TILE :])
        if k % 2 == 0:
            later = slice((k + 1) * TILE, (k + 2) * TILE)
            a_ref[later, later.start :] -= mm(a_ref[here, later], a_ref[here, later.start :], TN)
        else:
            pair = slice((k - 1) * TILE, (k + 1) * TILE)
            for i in range(k + 1, nb, 2):
                later = slice(i * TILE, (i + 2) * TILE)
                a_ref[later, i * TILE :] -= mm(a_ref[pair, later], a_ref[pair, i * TILE :], TN)

    def step(k, carry):
        at = pl.multiple_of(k * TILE, TILE)
        G = factor_tile([a_ref[pl.ds(at + 8 * q, 8), pl.ds(at, TILE)] for q in range(TILE // 8)], zero)
        for q in range(TILE // 8):
            g_ref[k, 8 * q : 8 * q + 8, :] = G[q]
        to = pl.ds(pl.multiple_of(k * wide, wide), wide)
        rows = rows_ref[:, to]
        sq = jnp.sum(rows * rows * weight_ref[:, 0:1], axis=0, keepdims=True)
        kern_ref[:, to] = jnp.exp(dot16(left_ref[...], right_terms(rows, sq, 0), NN))
        lax.switch(k, [functools.partial(after_tile, i) for i in range(nb)])
        return carry

    lax.fori_loop(0, nb, step, 0)

    for k in range(nb):
        cols = slice(k * TILE, (k + 1) * TILE)
        r = lax.broadcasted_iota(jnp.int32, (share, TILE), 0) + col * share
        c = lax.broadcasted_iota(jnp.int32, (share, TILE), 1) + k * TILE
        b_ref[0:share, cols] = jnp.where(r == c, 1.0, 0.0).astype(jnp.float32)
        b_ref[share : 2 * share, cols] = a_ref[cols, B : B + TILE].T[0:share, :]
    for k in range(nb - 1, -1, -1):
        cols = slice(k * TILE, (k + 1) * TILE)
        z = stacked(b_ref[:, cols], g_ref[k])
        z_ref[:, cols] = z
        if k > 0:
            b_ref[:, 0 : k * TILE] = b_ref[:, 0 : k * TILE] - stacked(z, a_ref[0 : k * TILE, cols], NT)

    own = pl.ds(pl.multiple_of(col * share, share), share)
    to = pl.multiple_of(row * TILE, TILE)
    tile = a_ref[own, pl.ds(to, TILE)]
    r = lax.broadcasted_iota(jnp.int32, (share, TILE), 0) + col * share
    c = lax.broadcasted_iota(jnp.int32, (share, TILE), 1) + to
    diag_ref[...] = jnp.where(c >= r, tile, 0.0)

    block = 2 * wide

    def product(j, carry):
        to = pl.ds(pl.multiple_of(j * block, block), block)
        both = stacked(z_ref[...], kern_ref[0:B, to])
        panel_ref[:, to] = both[0:share]
        update_ref[:, to] = kern_ref[B : B + share, to] - both[share : 2 * share]
        return carry

    lax.fori_loop(0, rows_ref.shape[1] // block, product, 0)


def pack(points, copies):
    rows = jnp.broadcast_to(points.T, (copies,) + points.shape[::-1])
    return jnp.concatenate([rows[:, 0:16], rows[:, 16:32]], axis=2)


def local(panel, look, sent_look, scales, row_points):
    share = 2 * look.shape[0]
    rows_dev = row_points.shape[1]
    vmem = pl.BlockSpec(memory_space=pltpu.VMEM)
    out = jax.ShapeDtypeStruct((share, rows_dev), jnp.float32)
    diag, panel_tile, updated = pl.pallas_call(
        panel_kernel,
        out_shape=(jax.ShapeDtypeStruct((share, B // 8), jnp.float32), out, out),
        in_specs=[vmem] * 5,
        out_specs=(vmem, vmem, vmem),
        scratch_shapes=[
            pltpu.VMEM((2 * share, B), jnp.float32),
            pltpu.VMEM((B + share, 4 * TILE), jnp.bfloat16),
            pltpu.VMEM((B, B + TILE), jnp.float32),
            pltpu.VMEM((B // TILE, TILE, TILE), jnp.float32),
            pltpu.VMEM((2 * share, B), jnp.float32),
            pltpu.VMEM((B + TILE, 4 * TILE), jnp.bfloat16),
            pltpu.VMEM((B + share, rows_dev), jnp.float32),
            pltpu.VMEM((F, TILE), jnp.float32),
        ],
        name="panel",
    )(panel, look, sent_look, scales.reshape(1, F), row_points)
    return (diag.T, panel_tile, updated)


def body(row_points, panel_points, scales):
    n_col = lax.axis_size("col")
    n_row = lax.axis_size("row")
    col = lax.axis_index("col")
    row = lax.axis_index("row")
    share = B // n_col
    rows_dev = row_points.shape[1]
    first = col * share
    panel = lax.all_to_all(pack(panel_points, n_col), "col", 0, 0, tiled=True)
    panel = panel.reshape(B // 2, 2 * F)
    look = pack(lax.dynamic_slice_in_dim(row_points, first % rows_dev, share, 1), 1)[0]
    sent = [lax.ppermute(look, "row", [(0, to)]) for to in range(n_row - 2, 0, -2)]
    look = jnp.where(row == 0, look, sum(sent[1:], sent[0]))
    next_row = lax.ppermute(look, "row", [(i, i + 1) for i in range(0, n_row, 2)])
    return local(panel, look, next_row, scales, row_points)


def solution(mesh):
    return jax.shard_map(
        body,
        mesh=mesh,
        in_specs=(P(None, "row"), P(None, "col"), P()),
        out_specs=(P("row", "col"), P("col", "row"), P("col", "row")),
        check_vma=False,
    )
```

```python
import functools

import jax
import jax.numpy as jnp
from jax import lax
from jax.experimental import pallas as pl
from jax.experimental.pallas import tpu as pltpu
from jax.sharding import PartitionSpec as P

B = 1024
F = 64
RIDGE = 0.5
TILE = 128
REG = (8, 128)
NEAR = 4
NN = ((1,), (0,))
TN = ((0,), (0,))
NT = ((1,), (1,))


def mm(a, b, dims):
    return lax.dot_general(
        a, b, (dims, ((), ())), precision=lax.Precision.HIGHEST, preferred_element_type=jnp.float32
    )


def row_all(x, i):
    return jnp.broadcast_to(x[i : i + 1, :], REG)


def col_all(x, j):
    return jnp.broadcast_to(x[:, j : j + 1], REG)


def tree_sum(xs):
    xs=list(xs)
    while len(xs)>1:
        xs=[xs[i]+xs[i+1] if i+1<len(xs) else xs[i] for i in range(0,len(xs),2)]
    return xs[0]

def small_chol(d):
    d=list(d)
    rs=[None]*8; l=[[None]*8 for _ in range(8)]
    for s in range(0,8,2):
        a,b,c=row_all(d[s],s),row_all(d[s],s+1),row_all(d[s+1],s+1)
        det=a*c-b*b
        r0=lax.rsqrt(a); rd=lax.rsqrt(det); inv=rd*rd
        rs[s]=r0; rs[s+1]=(a*r0)*rd
        y1=a*d[s+1]-b*d[s]
        l0=d[s]*r0; l1=y1*(r0*rd)
        for k in range(s+1,8): l[k][s]=row_all(l0,k)
        for k in range(s+2,8): l[k][s+1]=row_all(l1,k)
        if s<6:
            y0=c*d[s]-b*d[s+1]
            for m in range(s+2,8):
                d[m]=d[m]-(y0*row_all(d[s],m)+y1*row_all(d[s+1],m))*inv
    return rs,l
def forward(x,rs,l):
    x=list(x)
    for s in range(8):
        x[s]=x[s]*rs[s]
        for k in range(s+1,8): x[k]=x[k]-l[k][s]*x[s]
    return x
def backward(x,rs,l):
    x=list(x)
    for s in range(7,-1,-1):
        x[s]=x[s]*rs[s]
        for k in range(s): x[k]=x[k]-l[s][k]*x[s]
    return x

def factor_tile(W, zero):
    n=len(W); W=list(W)
    sub=lax.broadcasted_iota(jnp.int32,REG,0); lane=lax.broadcasted_iota(jnp.int32,REG,1)
    G=[None]*n
    def finish(p, rs, l):
        mine=lax.shift_right_logical(lane,3)==p
        w=jnp.where(mine, jnp.where(lane-8*p==sub,1.0,0.0).astype(jnp.float32), W[p])
        w=forward([row_all(w,s) for s in range(8)],rs,l)
        g=w[7]
        for s in range(6,-1,-1): g=jnp.where(sub==s,w[s],g)
        G[p]=jnp.where(lane<8*(p+1),g,0.0)
        return mine,w
    for t in range(n//2):
        p0,p1=2*t,2*t+1
        near=range(p1+1,min(p1+1+NEAR,n)); far=range(min(p1+1+NEAR,n),n)
        c0={p0:[],p1:[]}
        for k in range(8):
            c0[p0].append(col_all(W[p0],8*p0+k)); c0[p1].append(col_all(W[p1],8*p0+k))
        d1=[col_all(W[p1],8*p1+k) for k in range(8)]
        c0.update({q:[col_all(W[q],8*p0+k) for k in range(8)] for q in near})
        old=list(W)
        rs,l=small_chol([x+zero for x in c0[p0]])
        x=forward(c0[p1],rs,l)
        d1=[d1[k]-tree_sum([x[s]*row_all(x[s],k) for s in range(8)]) for k in range(8)]
        mine0,w=finish(p0,rs,l)
        W[p1]=jnp.where(mine0,0.0,W[p1])-tree_sum([x[s]*w[s] for s in range(8)])
        v0=backward(w,rs,l)
        for q in near:
            W[q]=jnp.where(mine0,0.0,W[q])-tree_sum([c0[q][s]*v0[s] for s in range(8)])
        rs,l=small_chol(d1)
        c1={q:[col_all(W[q],8*p1+k) for k in range(8)] for q in near}
        mine1,w=finish(p1,rs,l)
        v1=backward(w,rs,l)
        for q in near:
            W[q]=jnp.where(mine1,0.0,W[q])-tree_sum([c1[q][s]*v1[s] for s in range(8)])
        if len(far):
            def pick(v):
                o=v[7]
                for s in range(6,-1,-1): o=jnp.where(sub==s,v[s],o)
                return o
            V0=pick(v0); V1=pick(v1)
            V0=jnp.where(mine1,0.0,V0)-tree_sum([col_all(V0,8*p1+k)*v1[k] for k in range(8)])
            z=jnp.zeros(REG,jnp.float32)
            rhs=jnp.concatenate([z]*p0+[V0,V1]+[z]*(n-p1-1),0)
            prod=lax.dot_general(jnp.concatenate([old[q] for q in far],0),rhs,(((1,),(0,)),((),())),precision=lax.Precision.HIGHEST,preferred_element_type=jnp.float32)
            for i,q in enumerate(far):
                W[q]=jnp.where(mine0|mine1,0.0,W[q])-prod[8*i:8*i+8]
    return G


def unpack_points(packed):
    n = packed.shape[0] // 16
    halves = packed.reshape(n, 16, 2 * F)
    return jnp.concatenate([halves[:, :, :F], halves[:, :, F:]], axis=1).reshape(32 * n, F)


def split(x):
    high = x.astype(jnp.bfloat16)
    rest = x - high.astype(jnp.float32)
    middle = rest.astype(jnp.bfloat16)
    low = (rest - middle.astype(jnp.float32)).astype(jnp.bfloat16)
    return high, middle, low


def stacked(a, b, dims=NN):
    n = a.shape[0]
    high, middle, low = split(a)
    b = split(b)
    first = dot16(jnp.concatenate([high, middle, low], axis=0), b[0], dims)
    second = dot16(jnp.concatenate([high, middle], axis=0), b[1], dims)
    small = first[2 * n :] + second[n:] + dot16(high, b[2], dims)
    return first[0:n] + (first[n : 2 * n] + second[0:n] + small)


def chained(a, b):
    a, b = split(a), split(b)
    left = jnp.concatenate([a[i] for i in (0, 0, 1, 1, 0, 2)], axis=1)
    right = jnp.concatenate([b[i] for i in (0, 1, 0, 1, 2, 0)], axis=0)
    return dot16(left, right, NN)


def spread_terms(parts, order, values, first_one, axis):
    shape = list(parts[0].shape)
    shape[axis] = TILE
    place = lax.broadcasted_iota(jnp.int32, shape, axis)
    tail = jnp.where((place >= first_one) & (place < first_one + 3), 1.0, 0.0).astype(jnp.float32)
    for i, v in enumerate(values):
        tail = jnp.where(place == 3 - first_one + i, v, tail)
    return jnp.concatenate([parts[i] for i in order] + [tail.astype(jnp.bfloat16)], axis=axis)


def as_float(parts):
    return [p.astype(jnp.float32) for p in parts]


LEFT = (0, 0, 1, 0, 1, 2)
RIGHT = (0, 1, 0, 2, 1, 0)


def left_terms(points, scales):
    weighted = points * scales
    sq = jnp.sum(weighted * points, axis=1, keepdims=True)
    return spread_terms(split(2.0 * weighted), LEFT, as_float(split(-sq)), 3, 1)


def right_terms(points, sq, axis):
    return spread_terms(split(points), RIGHT, as_float(split(-sq)), 0, axis)


def dot16(a, b, dims):
    return lax.dot_general(a, b, (dims, ((), ())), preferred_element_type=jnp.float32)


def panel_kernel(
    pan_ref, look_ref, sent_ref, scales_ref, rows_ref,
    diag_ref, panel_ref, update_ref,
    z_ref, left_ref, a_ref, g_ref, b_ref, right_ref, kern_ref, weight_ref,
):
    nb = B // TILE
    col, row = lax.axis_index("col"), lax.axis_index("row")
    scales = scales_ref[...]
    weight_ref[...] = jnp.broadcast_to(jnp.broadcast_to(scales, (8, F)).T[:, 0:1], (F, TILE))
    zero = jnp.full(REG, jnp.minimum(col, 0).astype(jnp.float32))
    points = unpack_points(pan_ref[...])
    look = unpack_points(jnp.where(row % 2 == 0, look_ref[...], sent_ref[...]))
    share = look.shape[0]
    left_ref[0:B] = left_terms(points, scales)
    left_ref[B : B + share] = left_terms(look, scales)
    others = jnp.concatenate([points, look, jnp.zeros((TILE - share, F), jnp.float32)], axis=0)
    right_ref[...] = right_terms(others, jnp.sum(others * others * scales, axis=1, keepdims=True), 1)
    for i in range(nb):
        at = slice(i * TILE, (i + 1) * TILE)
        block = jnp.exp(dot16(left_ref[at], right_ref[i * TILE :], NT))
        a_ref[at, i * TILE :] = block
        rid = lax.broadcasted_iota(jnp.int32, (TILE, TILE), 0)
        cid = lax.broadcasted_iota(jnp.int32, (TILE, TILE), 1)
        a_ref[at, at] = jnp.where(rid == cid, block[:, 0:TILE] + RIDGE, block[:, 0:TILE])
        if i % 2 == 1:
            a_ref[at, (i - 1) * TILE : i * TILE] = jnp.zeros((TILE, TILE), jnp.float32)

    wide = rows_ref.shape[1] // nb

    def after_tile(k):
        here = slice(k * TILE, (k + 1) * TILE)
        a_ref[here, k * TILE :] = chained(g_ref[k], a_ref[here, k * TILE :])
        if k % 2 == 0:
            later = slice((k + 1) * TILE, (k + 2) * TILE)
            a_ref[later, later.start :] -= mm(a_ref[here, later], a_ref[here, later.start :], TN)
        else:
            pair = slice((k - 1) * TILE, (k + 1) * TILE)
            for i in range(k + 1, nb, 2):
                later = slice(i * TILE, (i + 2) * TILE)
                a_ref[later, i * TILE :] -= mm(a_ref[pair, later], a_ref[pair, i * TILE :], TN)

    def step(k, carry):
        at = pl.multiple_of(k * TILE, TILE)
        G = factor_tile([a_ref[pl.ds(at + 8 * q, 8), pl.ds(at, TILE)] for q in range(TILE // 8)], zero)
        for q in range(TILE // 8):
            g_ref[k, 8 * q : 8 * q + 8, :] = G[q]
        to = pl.ds(pl.multiple_of(k * wide, wide), wide)
        rows = rows_ref[:, to]
        sq = jnp.sum(rows * rows * weight_ref[:, 0:1], axis=0, keepdims=True)
        kern_ref[:, to] = jnp.exp(dot16(left_ref[...], right_terms(rows, sq, 0), NN))
        lax.switch(k, [functools.partial(after_tile, i) for i in range(nb)])
        return carry

    lax.fori_loop(0, nb, step, 0)

    for k in range(nb):
        cols = slice(k * TILE, (k + 1) * TILE)
        r = lax.broadcasted_iota(jnp.int32, (share, TILE), 0) + col * share
        c = lax.broadcasted_iota(jnp.int32, (share, TILE), 1) + k * TILE
        b_ref[0:share, cols] = jnp.where(r == c, 1.0, 0.0).astype(jnp.float32)
        b_ref[share : 2 * share, cols] = a_ref[cols, B : B + TILE].T[0:share, :]
    for k in range(nb - 1, -1, -1):
        cols = slice(k * TILE, (k + 1) * TILE)
        z = stacked(b_ref[:, cols], g_ref[k])
        z_ref[:, cols] = z
        if k > 0:
            b_ref[:, 0 : k * TILE] = b_ref[:, 0 : k * TILE] - stacked(z, a_ref[0 : k * TILE, cols], NT)

    own = pl.ds(pl.multiple_of(col * share, share), share)
    to = pl.multiple_of(row * TILE, TILE)
    tile = a_ref[own, pl.ds(to, TILE)]
    r = lax.broadcasted_iota(jnp.int32, (share, TILE), 0) + col * share
    c = lax.broadcasted_iota(jnp.int32, (share, TILE), 1) + to
    diag_ref[...] = jnp.where(c >= r, tile, 0.0)

    block = 2 * wide

    def product(j, carry):
        to = pl.ds(pl.multiple_of(j * block, block), block)
        both = stacked(z_ref[...], kern_ref[0:B, to])
        panel_ref[:, to] = both[0:share]
        update_ref[:, to] = kern_ref[B : B + share, to] - both[share : 2 * share]
        return carry

    lax.fori_loop(0, rows_ref.shape[1] // block, product, 0)


def pack(points, copies):
    rows = jnp.broadcast_to(points.T, (copies,) + points.shape[::-1])
    return jnp.concatenate([rows[:, 0:16], rows[:, 16:32]], axis=2)


def local(panel, look, sent_look, scales, row_points):
    share = 2 * look.shape[0]
    rows_dev = row_points.shape[1]
    vmem = pl.BlockSpec(memory_space=pltpu.VMEM)
    out = jax.ShapeDtypeStruct((share, rows_dev), jnp.float32)
    diag, panel_tile, updated = pl.pallas_call(
        panel_kernel,
        out_shape=(jax.ShapeDtypeStruct((share, B // 8), jnp.float32), out, out),
        in_specs=[vmem] * 5,
        out_specs=(vmem, vmem, vmem),
        scratch_shapes=[
            pltpu.VMEM((2 * share, B), jnp.float32),
            pltpu.VMEM((B + share, 4 * TILE), jnp.bfloat16),
            pltpu.VMEM((B, B + TILE), jnp.float32),
            pltpu.VMEM((B // TILE, TILE, TILE), jnp.float32),
            pltpu.VMEM((2 * share, B), jnp.float32),
            pltpu.VMEM((B + TILE, 4 * TILE), jnp.bfloat16),
            pltpu.VMEM((B + share, rows_dev), jnp.float32),
            pltpu.VMEM((F, TILE), jnp.float32),
        ],
        name="panel",
    )(panel, look, sent_look, scales.reshape(1, F), row_points)
    return (diag.T, panel_tile, updated)


def body(row_points, panel_points, scales):
    n_col = lax.axis_size("col")
    n_row = lax.axis_size("row")
    col = lax.axis_index("col")
    row = lax.axis_index("row")
    share = B // n_col
    rows_dev = row_points.shape[1]
    first = col * share
    panel = lax.all_to_all(pack(panel_points, n_col), "col", 0, 0, tiled=True)
    panel = panel.reshape(B // 2, 2 * F)
    look = pack(lax.dynamic_slice_in_dim(row_points, first % rows_dev, share, 1), 1)[0]
    sent = [lax.ppermute(look, "row", [(0, to)]) for to in range(n_row - 2, 0, -2)]
    look = jnp.where(row == 0, look, sum(sent[1:], sent[0]))
    next_row = lax.ppermute(look, "row", [(i, i + 1) for i in range(0, n_row, 2)])
    return local(panel, look, next_row, scales, row_points)


def solution(mesh):
    return jax.shard_map(
        body,
        mesh=mesh,
        in_specs=(P(None, "row"), P(None, "col"), P()),
        out_specs=(P("row", "col"), P("col", "row"), P("col", "row")),
        check_vma=False,
    )
```
